256 devices in a mesh: px: 32 (over y, z), py: 8 (over x, core).
Axes of the slice: x: 4, y: 4, z: 8, core: 2. Of those that a mesh axis runs over, the one named last changes fastest.
Arguments:
- eta_boxes: float32 [1024, 32, 32, 128], P(('px', 'py')), may hold values from 0 to 1
- corners: int32 [1024, 2], P(('px', 'py')), may hold values from 0 to 95, as said below
- grain_ids: int32 [1024], P(('px', 'py')), may hold values from 0 to 23
- misfit: float32 [24], replicated, may hold values from -1 to 1
- green: float32 [128, 768, 512], P('px', 'py'), may hold values from 0.25 to 2.5
Outputs:
- eta_next: float32 [1024, 32, 32, 128], P(('px', 'py'))
- potential: float32 [768, 512, 128], P('px', 'py')
The draws below stay inside these ranges and needn't reach their ends.
Inputs may be any that keep to these rules, and one draw needn't show every extreme that they name: Box b lies with device d = b // 4 (px index p = d // 8, py index q = d % 8): 8 corners[b,0] lies in [p * 24, (p + 1) * 24) and 8 corners[b,1] in [q * 64, (q + 1) * 64). Among each device's boxes one has its corner at the last tile grid position of that device's cells in both columns.
All inputs are finite; a program needn't handle non-finite values.
Results may differ from the reference program's by a relative error of at most 0.000075.
Values sent between devices are 32-bit elements; how exact they have to be, the bound alone decides.
A program may use at most 64 MiB of HBM per device.

```python
import math
import jax
import jax.numpy as jnp
from jax import lax

NX = 768
NY = 512
NZ = 128
BX = 32
BY = 32
STEP = 8
VARIANTS = 24
BOX_DEV = 4
CX = 24
CY = 64
BOXES = 1024


def draw_corners(key, part):
    owner = jnp.arange(BOXES, dtype=jnp.int32) // BOX_DEV
    slot_index = jnp.arange(BOXES, dtype=jnp.int32) % BOX_DEV
    devices_y = NY // CY
    row_dev = owner // devices_y
    col_dev = owner % devices_y
    steps_x = CX // STEP
    steps_y = CY // STEP
    first_key = jax.random.fold_in(key, 11)
    second_key = jax.random.fold_in(key, 12)
    third_key = jax.random.fold_in(key, 13)
    offset_x = jax.random.randint(first_key, (BOXES,), 0, steps_x, dtype=jnp.int32)
    offset_y = jax.random.randint(second_key, (BOXES,), 0, steps_y, dtype=jnp.int32)
    chosen = jax.random.randint(third_key, (BOXES // BOX_DEV,), 0, BOX_DEV, dtype=jnp.int32)
    forced = slot_index == chosen[owner]
    offset_x = jnp.where(forced, steps_x - 1, offset_x)
    offset_y = jnp.where(forced, steps_y - 1, offset_y)
    corner_x = row_dev * steps_x + offset_x
    corner_y = col_dev * steps_y + offset_y
    return jnp.stack([corner_x, corner_y], axis=1).astype(jnp.int32)


def with_ends(array, key, low, largest):
    index_at = [jax.random.randint(jax.random.fold_in(key, axis), (), 0, length) for axis, length in enumerate(array.shape)]
    main_axis = array.shape.index(max(array.shape))
    beside = index_at[:main_axis] + [(index_at[main_axis] + 1) % array.shape[main_axis]] + index_at[main_axis + 1:]
    return array.at[tuple(index_at)].set(low).at[tuple(beside)].set(largest)


def levels(stream_key, extent, cuts, least, largest):
    gain, own = 1.0, jax.random.fold_in(stream_key, 6)
    for dim, parts in cuts:
        heights = jnp.exp(jax.random.uniform(jax.random.fold_in(own, dim), (parts,), jnp.float32, least / len(cuts), largest / len(cuts)))
        gain = gain * jnp.repeat(heights, extent[dim] // parts).reshape([-1 if axis == dim else 1 for axis in range(len(extent))])
    return gain


def setup_inputs(seed: int = 0) -> dict:
    key_of = jax.random.split(jax.random.key(seed), 6)
    return {
        "eta_boxes": jnp.clip(1.0 * jax.random.uniform(key_of[0], (BOXES, BX, BY, NZ), jnp.float32) ** levels(key_of[0], (BOXES, BX, BY, NZ), ((0, 256),), -0.2, 0.2), 0.0, 1.0),
        "corners": draw_corners(jax.random.fold_in(key_of[5], 71), 0),
        "grain_ids": with_ends(jax.random.randint(key_of[2], (BOXES,), 0, VARIANTS), jax.random.fold_in(key_of[2], 1), 0, VARIANTS - 1).astype(jnp.int32),
        "misfit": jnp.clip(jax.random.uniform(key_of[3], (VARIANTS,), jnp.float32, -1.0, 1.0), -1.0, 1.0),
        "green": jnp.clip(jnp.exp(math.log(2.5) - 2.3025851 * jax.random.uniform(key_of[4], (NZ, NX, NY), jnp.float32) ** levels(key_of[4], (NZ, NX, NY), ((0, 32), (1, 8)), -0.2, 0.2)), 0.25, 2.5),
    }


rate_step = 0.2
gradient_coef = 0.1
coupling = 1.5


def laplace(values):
    padded = jnp.pad(values, ((1, 1), (1, 1), (0, 0)))
    beside_all = padded[2:, 1:-1] + padded[:-2, 1:-1] + padded[1:-1, 2:] + padded[1:-1, :-2]
    beside_all = beside_all + jnp.roll(values, 1, axis=2) + jnp.roll(values, -1, axis=2)
    return beside_all - 6.0 * values


def advance(order_param, weight, field_mu, occupancy):
    square = order_param * order_param
    force = order_param * square - order_param + 2.0 * coupling * order_param * (occupancy - square)
    force = force - gradient_coef * laplace(order_param) + 2.0 * weight * order_param * field_mu
    return order_param - rate_step * force


def reference(eta_boxes, corners, grain_ids, misfit, green):
    weights = misfit[grain_ids]
    squares = eta_boxes * eta_boxes
    starts = (corners * STEP).astype(jnp.int32)
    anchor_zero = jnp.zeros((), jnp.int32)
    canvas = jnp.zeros((2, NX + BX, NY + BY, NZ), jnp.float32)

    def place(running, inputs):
        square, weight, anchor = inputs
        contrib = jnp.stack([weight * square, square])
        position = (anchor_zero, anchor[0], anchor[1], anchor_zero)
        current = lax.dynamic_slice(running, position, contrib.shape)
        return lax.dynamic_update_slice(running, current + contrib, position), None

    canvas, unused = lax.scan(place, canvas, (squares, weights, starts))
    folded = canvas[:, :NX, :NY]
    folded = folded.at[:, :BX].add(canvas[:, NX:, :NY])
    folded = folded.at[:, :, :BY].add(canvas[:, :NX, NY:])
    folded = folded.at[:, :BX, :BY].add(canvas[:, NX:, NY:])
    multiplier = jnp.transpose(green, (1, 2, 0))
    spectrum = jnp.fft.fftn(folded[0]) * multiplier
    potential = jnp.real(jnp.fft.ifftn(spectrum)).astype(jnp.float32)
    stacked = jnp.stack([potential, folded[1]])
    wrapped = jnp.pad(stacked, ((0, 0), (0, BX), (0, BY), (0, 0)), mode="wrap")

    def update(inputs):
        order_param, weight, anchor = inputs
        position = (anchor_zero, anchor[0], anchor[1], anchor_zero)
        window_vals = lax.dynamic_slice(wrapped, position, (2, BX, BY, NZ))
        return advance(order_param, weight, window_vals[0], window_vals[1])

    eta_next = lax.map(update, (eta_boxes, weights, starts))
    return eta_next, potential
```

```python
import functools

import jax
import jax.numpy as jnp
import numpy as np
from jax import lax
from jax.experimental import pallas as pl
from jax.experimental.pallas import tpu as pltpu
from jax.sharding import PartitionSpec as P

NX, NY, NZ = 768, 512, 128
STEP = 8
PX, PY = 32, 8
CX, CY = NX // PX, NY // PY
OV = 24
KX = NX // PY
F32 = jnp.float32
BF16 = jnp.bfloat16
SPECIAL = 16
RATE = 0.2
GRADIENT = 0.1
COUPLING = 1.5

VM = pl.BlockSpec(memory_space=pltpu.VMEM)
SM = pl.BlockSpec(memory_space=pltpu.SMEM)


def halves(array):
    high = np.asarray(array, np.float32).astype(jnp.bfloat16)
    low = (np.asarray(array, np.float64) - high.astype(np.float64)).astype(jnp.bfloat16)
    return high, low


def slot_wave(p, h):
    if h == 0:
        return 4 * p + 1
    return 4 * p + 2 if p < 16 else 4 * p


def depth_tables():
    z = np.arange(NZ)
    forward = np.zeros((NZ, NZ))
    inverse = np.zeros((NZ, NZ))
    total = NX * NY * NZ
    for h in range(2):
        for p in range(PX):
            row_re, row_im = h * 64 + p, h * 64 + 32 + p
            wave = slot_wave(p, h)
            cosine = np.cos(2 * np.pi * ((wave * z) % NZ) / NZ)
            sine = np.sin(2 * np.pi * ((wave * z) % NZ) / NZ)
            if p == SPECIAL and h == 1:
                forward[row_re], forward[row_im] = 1.0, (-1.0) ** z
                inverse[row_re], inverse[row_im] = 1.0 / total, (-1.0) ** z / total
            else:
                forward[row_re], forward[row_im] = cosine, -sine
                inverse[row_re], inverse[row_im] = 2 * cosine / total, -2 * sine / total
    return forward, inverse


def wave_rows(count, step, length):
    angle = 2 * np.pi * ((step * np.arange(count)[:, None] * np.arange(length)[None]) % length) / length
    return np.stack([np.cos(angle), np.sin(angle)]).astype(np.float32)


def column_tables():
    k = np.arange(NY)
    angle = 2 * np.pi * ((k[:, None] * k[None]) % NY) / NY
    return halves(np.concatenate([np.cos(angle), np.sin(angle)], axis=1))


def mirror_tables():
    rows = np.zeros((KX, KX), np.float32)
    for j in range(1, KX):
        rows[j, KX - j] = 1.0
    lanes = np.zeros((NY, NY), np.float32)
    for k in range(NY):
        lanes[(NY - k) % NY, k] = 1.0
    return rows.astype(jnp.bfloat16), lanes.astype(jnp.bfloat16)


def split(value):
    high = value.astype(BF16)
    return high, (value - high.astype(F32)).astype(BF16)


def dot(a, b):
    return jnp.dot(a, b, preferred_element_type=F32)


def dot3(a, b):
    return dot(a[0], b[0]) + dot(a[0], b[1]) + dot(a[1], b[0])


def turn(value):
    return pltpu.roll(value, 64, axis=value.ndim - 1)


def low_lanes(shape):
    return lax.broadcasted_iota(jnp.int32, shape, len(shape) - 1) < 64


def call(kernel, outs, specs, args, scratch=(), **params):
    return pl.pallas_call(
        kernel,
        out_shape=outs,
        in_specs=specs,
        out_specs=jax.tree.map(lambda unused: VM, outs),
        scratch_shapes=scratch,
        compiler_params=pltpu.CompilerParams(vmem_limit_bytes=60 * 1024 * 1024, **params),
    )(*args)


def shaped(*shape, dtype=F32):
    return jax.ShapeDtypeStruct(shape, dtype)


def place_kernel(start, ids, misfit, eta, own_e, next_e, side_e, corner_e, own_o, next_o, side_o, corner_o, field, cover):
    field[...] = jnp.zeros_like(field)
    cover[...] = jnp.zeros_like(cover)
    for b in range(eta.shape[0]):
        weight = misfit[ids[b]]
        sx = start[0, b]
        sy = pl.multiple_of(start[1, b], 8)

        def body(i, unused):
            value = eta[b, i]
            square = value * value
            rows = pl.ds(sy, 32)
            field[sx + i, rows, :] = field[sx + i, rows, :] + weight * square
            cover[sx + i, rows, :] = cover[sx + i, rows, :] + square
            return unused

        lax.fori_loop(0, 32, body, 0, unroll=4)
    for source, own, beside, side, corner in ((field, own_e, next_e, side_e, corner_e), (cover, own_o, next_o, side_o, corner_o)):
        own[...] = source[:CX, :CY]
        beside[...] = source[CX:, :CY]
        side[...] = source[:CX, CY:]
        corner[...] = source[CX:, CY:]


def gather_kernel(own, beside, side, corner, out, first):
    out[...] = own[...] + beside[...]
    out[:, :OV] = out[:, :OV] + (side[...] + corner[...])
    first[...] = out[:, :OV]


def depth_kernel(own, beside, side, corner, wave_h, wave_l, out, field):
    field[...] = own[...] + beside[...]
    field[:, :OV] = field[:, :OV] + (side[...] + corner[...])
    waves = (wave_h[...], wave_l[...])
    keep = low_lanes((PX, 128))
    nt = (((1,), (1,)), ((), ()))
    for group in range(CX // 4):
        rows = split(field[4 * group : 4 * group + 4].reshape(256, NZ))
        spectrum = (
            lax.dot_general(waves[0], rows[0], nt, preferred_element_type=F32)
            + lax.dot_general(waves[0], rows[1], nt, preferred_element_type=F32)
            + lax.dot_general(waves[1], rows[0], nt, preferred_element_type=F32)
        )
        for tile in range(2):
            for h in range(2):
                real = spectrum[64 * h : 64 * h + 32, 128 * tile : 128 * tile + 128]
                imag = spectrum[64 * h + 32 : 64 * h + 64, 128 * tile : 128 * tile + 128]
                x = 4 * group + 2 * tile
                out[pl.ds(24 * h + x, PX, stride=48), :] = jnp.where(keep, real, turn(imag))
                out[pl.ds(24 * h + x + 1, PX, stride=48), :] = jnp.where(keep, turn(real), imag)


def undepth_kernel(spectra, wave_h, wave_l, out, first):
    waves = (wave_h[...], wave_l[...])
    keep = low_lanes((PX, 128))
    for tile in range(CX // 2):
        x = 2 * tile
        parts = []
        for h in range(2):
            even = spectra[pl.ds(24 * h + x, PX, stride=48), :]
            odd = spectra[pl.ds(24 * h + x + 1, PX, stride=48), :]
            parts.append(jnp.where(keep, even, turn(odd)))
            parts.append(jnp.where(keep, turn(even), odd))
        block = split(jnp.concatenate(parts, axis=0).T)
        out[x : x + 2] = dot3(block, waves).reshape(2, CY, NZ)
    first[...] = out[:, :OV]


def table_kernel(coarse, fine, cos_h, cos_l, sin_h, sin_l):
    fine_c, fine_s = fine[0], fine[1]

    def body(k, unused):
        coarse_c, coarse_s = coarse[0, pl.ds(k, 1), :], coarse[1, pl.ds(k, 1), :]
        rows = pl.ds(pl.multiple_of(32 * k, 32), 32)
        cos_h[rows, :], cos_l[rows, :] = split(coarse_c * fine_c - coarse_s * fine_s)
        sin_h[rows, :], sin_l[rows, :] = split(coarse_s * fine_c + coarse_c * fine_s)
        return unused

    lax.fori_loop(0, NX // 32, body, 0)


def rows_kernel(place, lines, cos_h, cos_l, sin_h, sin_l, out):
    data = split(jnp.concatenate([lines[:, 0].reshape(NX, 128), lines[:, 1].reshape(NX, 128)], axis=1))
    keep = low_lanes((KX, 128))
    special = place[0] == SPECIAL
    for q in range(PY):
        rows = slice(KX * q, KX * q + KX)
        cosine = dot3((cos_h[rows], cos_l[rows]), data)
        sine = dot3((sin_h[rows], sin_l[rows]), data)
        for h in range(2):
            real, imag = cosine[:, 128 * h : 128 * h + 128], sine[:, 128 * h : 128 * h + 128]
            turned = turn(imag)
            normal = jnp.where(keep, real + turned, real - turned)
            if h == 1:
                if q < 4:
                    parted = jnp.where(keep, real, -turned)
                else:
                    parted = jnp.where(keep, turn(real), -imag)
                if q % 4 == 0:
                    parted = jnp.where(lax.broadcasted_iota(jnp.int32, (KX, 128), 0) == 0, real, parted)
                normal = jnp.where(special, parted, normal)
            out[q, h] = normal


def unrows_kernel(place, lines, cos_h, cos_l, sin_h, sin_l, out, one_h, one_l, two_h, two_l):
    keep = low_lanes((KX, 128))
    special = place[0] == SPECIAL
    for q in range(PY):
        rows = slice(KX * q, KX * q + KX)
        for h in range(2):
            value = lines[q, h]
            turned = turn(value)
            first = value
            second = jnp.where(keep, -turned, turned)
            if h == 1:
                if q < 4:
                    parted_1 = jnp.where(keep, 2.0 * value, 0.0)
                    parted_2 = jnp.where(keep, -2.0 * turned, 0.0)
                else:
                    parted_1 = jnp.where(keep, 0.0, 2.0 * turned)
                    parted_2 = jnp.where(keep, 0.0, -2.0 * value)
                if q % 4 == 0:
                    top = lax.broadcasted_iota(jnp.int32, (KX, 128), 0) == 0
                    parted_1 = jnp.where(top, value, parted_1)
                    parted_2 = jnp.where(top, 0.0, parted_2)
                first = jnp.where(special, parted_1, first)
                second = jnp.where(special, parted_2, second)
            lanes = slice(128 * h, 128 * h + 128)
            one_h[rows, lanes], one_l[rows, lanes] = split(first)
            two_h[rows, lanes], two_l[rows, lanes] = split(second)
    one = (one_h[...], one_l[...])
    two = (two_h[...], two_l[...])
    for block in range(8):
        rows = slice(96 * block, 96 * block + 96)
        result = dot3((cos_h[rows], cos_l[rows]), one) + dot3((sin_h[rows], sin_l[rows]), two)
        for h in range(2):
            out[4 * block : 4 * block + 4, h] = result[:, 128 * h : 128 * h + 128].reshape(4, CX, 128)


def green_kernel(place, own, near, far, extra, near_row, far_row, extra_row, row_flip, lane_flip, out, out_extra):
    p, q = place[0], place[1]
    special = p == SPECIAL
    upper = special & (q >= 4)
    lower = special & (q < 4)
    flips = row_flip[...]
    lanes = lane_flip[...]

    def permute(value):
        high, low = split(value)
        return dot(high, lanes) + dot(low, lanes)

    def mirror(plane, row):
        high, low = split(plane)
        turned = dot(flips, high) + dot(flips, low)
        top = lax.broadcasted_iota(jnp.int32, turned.shape, 0) == 0
        return permute(jnp.where(top, jnp.broadcast_to(row, turned.shape), turned))

    out[0] = 0.5 * (own[1] + mirror(near[...], near_row[0:1]))
    base = jnp.where(p < 16, own[2], jnp.where(lower, extra[...], own[0]))
    plane = jnp.where(upper, extra[...], far[...])
    row = jnp.where(upper, extra_row[0:1], far_row[0:1])
    second = 0.5 * (base + mirror(plane, row))
    packed = jnp.concatenate([jnp.broadcast_to(far_row[0:1], (8, NY)), jnp.broadcast_to(own[0, 0:1], (8, NY))], axis=0)
    packed = 0.5 * (packed + permute(packed))
    top = (lax.broadcasted_iota(jnp.int32, (KX, NY), 0) == 0) & special & (q % 4 == 0)
    out[1] = jnp.where(top, jnp.broadcast_to(packed[0:1], (KX, NY)), second)
    out_extra[...] = packed[8:16]


def columns_kernel(place, lines, green, green_extra, table_h, table_l, out, work_h, work_l):
    keep = low_lanes((KX, 128))
    packed = (place[0] == SPECIAL) & (place[1] % 4 == 0)
    for h in range(2):
        for tile in range(4):
            even, odd = lines[2 * tile, h], lines[2 * tile + 1, h]
            lanes = slice(128 * tile, 128 * tile + 128)
            rows = slice(192 * h, 192 * h + 96)
            work_h[rows, lanes], work_l[rows, lanes] = split(jnp.where(keep, even, turn(odd)))
            rows = slice(192 * h + 96, 192 * h + 192)
            work_h[rows, lanes], work_l[rows, lanes] = split(jnp.where(keep, turn(even), odd))
    tables = (table_h[...], table_l[...])
    wave = dot3((work_h[0:384], work_l[0:384]), tables)
    top = (lax.broadcasted_iota(jnp.int32, (KX, NY), 0) == 0) & packed
    for h in range(2):
        re_c, re_s = wave[192 * h : 192 * h + 96, :NY], wave[192 * h : 192 * h + 96, NY:]
        im_c, im_s = wave[192 * h + 96 : 192 * h + 192, :NY], wave[192 * h + 96 : 192 * h + 192, NY:]
        real, imag = re_c + im_s, im_c - re_s
        if h == 1:
            real, imag = jnp.where(top, re_c, real), jnp.where(top, -re_s, imag)
            fix = green_extra[...]
            work_h[384:392], work_l[384:392] = split(fix * im_c[0:8])
            work_h[392:400], work_l[392:400] = split(fix * -im_s[0:8])
        work_h[192 * h : 192 * h + 96], work_l[192 * h : 192 * h + 96] = split(green[h] * real)
        work_h[192 * h + 96 : 192 * h + 192], work_l[192 * h + 96 : 192 * h + 192] = split(green[h] * imag)
    wave = dot3((work_h[...], work_l[...]), tables)
    for h in range(2):
        real = wave[192 * h : 192 * h + 96, :NY] - wave[192 * h + 96 : 192 * h + 192, NY:]
        imag = wave[192 * h + 96 : 192 * h + 192, :NY] + wave[192 * h : 192 * h + 96, NY:]
        if h == 1:
            fix = wave[384:392, :NY] - wave[392:400, NY:]
            imag = jnp.where(top, jnp.broadcast_to(fix[0:1], (KX, NY)), imag)
        for tile in range(4):
            lanes = slice(128 * tile, 128 * tile + 128)
            re, im = real[:, lanes], imag[:, lanes]
            out[2 * tile, h] = jnp.where(keep, re, turn(im))
            out[2 * tile + 1, h] = jnp.where(keep, turn(re), im)


def update_kernel(start, ids, misfit, eta, mu_own, mu_side, mu_next, mu_corner, oc_own, oc_side, oc_next, oc_corner, out, field, cover):
    for source, own, side, beside, corner in (
        (field, mu_own, mu_side, mu_next, mu_corner),
        (cover, oc_own, oc_side, oc_next, oc_corner),
    ):
        source[:CX, :CY] = own[...]
        source[:CX, CY:] = side[...]
        source[CX:, :CY] = beside[...]
        source[CX:, CY:] = corner[...]
    sublane = lax.broadcasted_iota(jnp.int32, (32, NZ), 0)
    for b in range(eta.shape[0]):
        weight = misfit[ids[b]]
        sx = start[0, b]
        sy = pl.multiple_of(start[1, b], 8)

        def body(i, unused):
            value = eta[b, i]
            before = jnp.where(i > 0, eta[b, jnp.maximum(i - 1, 0)], 0.0)
            after = jnp.where(i < 31, eta[b, jnp.minimum(i + 1, 31)], 0.0)
            above = jnp.where(sublane == 0, 0.0, pltpu.roll(value, 1, axis=0))
            below = jnp.where(sublane == 31, 0.0, pltpu.roll(value, 31, axis=0))
            lap = before + after + above + below + pltpu.roll(value, 1, axis=1) + pltpu.roll(value, 127, axis=1) - 6.0 * value
            mu = field[sx + i, pl.ds(sy, 32), :]
            total = cover[sx + i, pl.ds(sy, 32), :]
            square = value * value
            force = value * square - value + 2.0 * COUPLING * value * (total - square)
            force = force - GRADIENT * lap + 2.0 * weight * value * mu
            out[b, i] = value - RATE * force
            return unused

        lax.fori_loop(0, 32, body, 0, unroll=2)


def shift(value, axis, by):
    peers = lax.axis_size(axis)
    return lax.ppermute(value, axis, [(i, (i + by) % peers) for i in range(peers)])


def both(value, pairs):
    return lax.ppermute(value, ("px", "py"), [(a * PY + b, c * PY + d) for (a, b), (c, d) in pairs])


def exchange(value, axis):
    return lax.all_to_all(value, axis, split_axis=0, concat_axis=0, tiled=True)


def green_parts(green, p):
    devices = [(a, b) for a in range(PX) for b in range(PY)]

    def far_of(a):
        return 31 - a if a >= 16 else (32 - a if a else SPECIAL)

    far_plane = jnp.where(p < 16, green[0], green[2])
    near = both(green[3], [((a, b), (31 - a, 7 - b)) for a, b in devices])
    far = both(far_plane, [((a, b), (far_of(a), 7 - b)) for a, b in devices])
    extra = both(
        green[0],
        [((0, b), (SPECIAL, b)) for b in range(4)] + [((SPECIAL, 7 - b), (SPECIAL, b)) for b in range(4, 8)],
    )
    near_row = both(green[3, :8], [((a, b), (31 - a, (8 - b) % 8)) for a, b in devices])
    far_row = both(far_plane[:8], [((a, b), (far_of(a), (8 - b) % 8)) for a, b in devices])
    extra_row = both(green[0, :8], [((SPECIAL, 8 - b), (SPECIAL, b)) for b in range(5, 8)])
    return near, far, extra, near_row, far_row, extra_row


def on_device(eta, corners, grain_ids, misfit, green):
    p, q = lax.axis_index("px"), lax.axis_index("py")
    place = jnp.stack([p, q]).astype(jnp.int32)
    start = jnp.stack([corners[:, 0] * STEP - p * CX, corners[:, 1] * STEP - q * CY]).astype(jnp.int32)
    forward, inverse = depth_tables()
    coarse, fine = wave_rows(24, 32, NX), wave_rows(32, 1, NX)
    columns = column_tables()

    near, far, extra, near_row, far_row, extra_row = green_parts(green, p)
    piece = [shaped(CX, CY, NZ), shaped(CX, CY, NZ), shaped(CX, OV, NZ), shaped(CX, OV, NZ)]
    patch = (CX + OV, CY + OV, NZ)
    own_e, next_e, side_e, corner_e, own_o, next_o, side_o, corner_o = call(
        place_kernel, piece + piece, [SM, SM, SM, VM], (start, grain_ids, misfit, eta), scratch=[pltpu.VMEM(patch, F32)] * 2
    )
    tables = call(table_kernel, [shaped(NX, NX, dtype=BF16)] * 4, [VM] * 2, (coarse, fine))

    def summed(beside, side, corner):
        return shift(beside, "px", 1), shift(side, "py", 1), shift(shift(corner, "py", 1), "px", 1)

    got_e = summed(next_e, side_e, corner_e)
    lines = call(
        depth_kernel, shaped(PX * 48, 128), [VM] * 6, (own_e, *got_e, *halves(forward)), scratch=[pltpu.VMEM((CX, CY, NZ), F32)]
    )
    lines = exchange(lines.reshape(PX, 2, CX, 128), "px")
    lines = call(rows_kernel, shaped(PY, 2, KX, 128), [SM] + [VM] * 5, (place, lines, *tables))
    lines = exchange(lines, "py")
    symmetric, symmetric_extra = call(
        green_kernel,
        [shaped(2, KX, NY), shaped(8, NY)],
        [SM] + [VM] * 9,
        (place, green, near, far, extra, near_row, far_row, extra_row, *mirror_tables()),
    )
    lines = call(
        columns_kernel,
        shaped(PY, 2, KX, 128),
        [SM] + [VM] * 5,
        (place, lines, symmetric, symmetric_extra, *columns),
        scratch=[pltpu.VMEM((400, NY), BF16)] * 2,
    )
    lines = exchange(lines, "py")
    lines = call(
        unrows_kernel,
        shaped(PX, 2, CX, 128),
        [SM] + [VM] * 5,
        (place, lines, *tables),
        scratch=[pltpu.VMEM((NX, 256), BF16)] * 4,
    )
    lines = exchange(lines, "px")
    potential, first = call(
        undepth_kernel,
        [shaped(CX, CY, NZ), shaped(CX, OV, NZ)],
        [VM] * 3,
        (lines.reshape(PX * 48, 128), *halves(inverse)),
    )

    def window(own, begin):
        side = shift(begin, "py", -1)
        return own, side, shift(own, "px", -1), shift(side, "px", -1)

    got_o = summed(next_o, side_o, corner_o)
    occupancy, first_o = call(gather_kernel, [shaped(CX, CY, NZ), shaped(CX, OV, NZ)], [VM] * 4, (own_o, *got_o))
    eta_next = call(
        update_kernel,
        shaped(*eta.shape),
        [SM] * 3 + [VM] * 9,
        (start, grain_ids, misfit, eta, *window(potential, first), *window(occupancy, first_o)),
        scratch=[pltpu.VMEM(patch, F32)] * 2,
    )
    return eta_next, potential


def solution(mesh):
    in_specs = (P(("px", "py"), None, None, None), P(("px", "py"), None), P(("px", "py")), P(), P("px", "py", None))
    out_specs = (P(("px", "py"), None, None, None), P("px", "py", None))
    return jax.shard_map(on_device, mesh=mesh, in_specs=in_specs, out_specs=out_specs, check_vma=False)
```

```python
import functools

import jax
import jax.numpy as jnp
import numpy as np
from jax import lax
from jax.experimental import pallas as pl
from jax.experimental.pallas import tpu as pltpu
from jax.sharding import PartitionSpec as P

NX, NY, NZ = 768, 512, 128
STEP = 8
PX, PY = 32, 8
CX, CY = NX // PX, NY // PY
OV = 24
KX = NX // PY
F32 = jnp.float32
BF16 = jnp.bfloat16
SPECIAL = 16
RATE = 0.2
GRADIENT = 0.1
COUPLING = 1.5

VM = pl.BlockSpec(memory_space=pltpu.VMEM)
SM = pl.BlockSpec(memory_space=pltpu.SMEM)


def halves(array):
    high = np.asarray(array, np.float32).astype(jnp.bfloat16)
    low = (np.asarray(array, np.float64) - high.astype(np.float64)).astype(jnp.bfloat16)
    return high, low


def slot_wave(p, h):
    if h == 0:
        return 4 * p + 1
    return 4 * p + 2 if p < 16 else 4 * p


def depth_tables():
    z = np.arange(NZ)
    forward = np.zeros((NZ, NZ))
    inverse = np.zeros((NZ, NZ))
    total = NX * NY * NZ
    for h in range(2):
        for p in range(PX):
            row_re, row_im = h * 64 + p, h * 64 + 32 + p
            wave = slot_wave(p, h)
            cosine = np.cos(2 * np.pi * ((wave * z) % NZ) / NZ)
            sine = np.sin(2 * np.pi * ((wave * z) % NZ) / NZ)
            if p == SPECIAL and h == 1:
                forward[row_re], forward[row_im] = 1.0, (-1.0) ** z
                inverse[row_re], inverse[row_im] = 1.0 / total, (-1.0) ** z / total
            else:
                forward[row_re], forward[row_im] = cosine, -sine
                inverse[row_re], inverse[row_im] = 2 * cosine / total, -2 * sine / total
    return forward, inverse


def wave_rows(count, step, length):
    angle = 2 * np.pi * ((step * np.arange(count)[:, None] * np.arange(length)[None]) % length) / length
    return np.stack([np.cos(angle), np.sin(angle)]).astype(np.float32)


def column_tables():
    k = np.arange(NY)
    angle = 2 * np.pi * ((k[:, None] * k[None]) % NY) / NY
    return halves(np.concatenate([np.cos(angle), np.sin(angle)], axis=1))


def mirror_tables():
    rows = np.zeros((KX, KX), np.float32)
    for j in range(1, KX):
        rows[j, KX - j] = 1.0
    lanes = np.zeros((NY, NY), np.float32)
    for k in range(NY):
        lanes[(NY - k) % NY, k] = 1.0
    return rows.astype(jnp.bfloat16), lanes.astype(jnp.bfloat16)


def split(value):
    high = value.astype(BF16)
    return high, (value - high.astype(F32)).astype(BF16)


def dot(a, b):
    return jnp.dot(a, b, preferred_element_type=F32)


def dot3(a, b):
    return dot(a[0], b[0]) + dot(a[0], b[1]) + dot(a[1], b[0])


def turn(value):
    return pltpu.roll(value, 64, axis=value.ndim - 1)


def low_lanes(shape):
    return lax.broadcasted_iota(jnp.int32, shape, len(shape) - 1) < 64


def call(kernel, outs, specs, args, scratch=(), **params):
    return pl.pallas_call(
        kernel,
        out_shape=outs,
        in_specs=specs,
        out_specs=jax.tree.map(lambda unused: VM, outs),
        scratch_shapes=scratch,
        compiler_params=pltpu.CompilerParams(vmem_limit_bytes=60 * 1024 * 1024, **params),
    )(*args)


def shaped(*shape, dtype=F32):
    return jax.ShapeDtypeStruct(shape, dtype)


def place_kernel(start, ids, misfit, eta, field, cover):
    field[...] = jnp.zeros_like(field)
    cover[...] = jnp.zeros_like(cover)
    for b in range(eta.shape[0]):
        weight = misfit[ids[b]]
        sx = start[0, b]
        sy = pl.multiple_of(start[1, b], 8)

        def body(i, unused):
            value = eta[b, i]
            square = value * value
            rows = pl.ds(sy, 32)
            field[sx + i, rows, :] = field[sx + i, rows, :] + weight * square
            cover[sx + i, rows, :] = cover[sx + i, rows, :] + square
            return unused

        lax.fori_loop(0, 32, body, 0, unroll=4)


MESH = pl.DeviceIdType.MESH
CUT_X = ((0, 12), (12, 36), (36, 48))
CUT_Y = ((0, 8), (8, 72), (72, 88))
LAND_X = ((12, 24), (0, 24), (0, 12))
LAND_Y = ((56, 64), (0, 64), (0, 16))
TAKE_X = ((0, 12), (0, 24), (12, 24))
TAKE_Y = ((0, 16), (0, 64), (56, 64))
GIVE_X = ((36, 48), (12, 36), (0, 12))
GIVE_Y = ((72, 88), (8, 72), (0, 8))
AROUND = [(a, b) for a, b in ((0, 1), (2, 1), (1, 0), (1, 2), (0, 0), (0, 2), (2, 0), (2, 2))]


def box(ref, x, y):
    return ref.at[pl.ds(x[0], x[1] - x[0]), pl.ds(y[0], y[1] - y[0])]


def wrap(value, count):
    return (value + count) % count


def push(source, target, send, receive, p, q):
    return pltpu.make_async_remote_copy(
        src_ref=source, dst_ref=target, send_sem=send, recv_sem=receive, device_id=(p, q), device_id_type=MESH
    )


def drain(ref, semaphore):
    pltpu.make_async_copy(ref, ref, semaphore).wait()


def mega_kernel(
    field, cover, green, coarse, fine, wave_h, wave_l, back_h, back_l, table_h, table_l, row_flip, lane_flip,
    mu_window, oc_window,
    grid, s1, r1, y1, t1, y2, t2, s2, r2, cos_h, cos_l, sin_h, sin_l,
    near, far, extra, near_row, far_row, extra_row, gs, gx, work_h, work_l, one_h, two_h, potential, occupancy,
    land_e, land_o, halo_send, halo_recv, green_send, green_recv, px_send, px_recv, py_send, py_recv,
):
    p, q = lax.axis_index("px"), lax.axis_index("py")
    upper_half = p // 16
    far_to = 31 - p + (1 - upper_half) - 16 * (1 - (p + 31) // 32)
    far_from = 31 - p + upper_half - 16 * upper_half * (1 - (p + 15) // 32)
    flip, flip_row = 7 - q, (8 - q) % 8

    barrier = pltpu.get_barrier_semaphore()

    def greet(a, b):
        pl.semaphore_signal(barrier, inc=1, device_id=(a, b), device_id_type=MESH)

    @pl.loop(1, PX)
    def _(j):
        greet((p + j) % PX, q)

    @pl.loop(1, PY)
    def _(j):
        greet(p, (q + j) % PY)

    for a in (-1, 1):
        for b in (-1, 1):
            greet(wrap(p + a, PX), wrap(q + b, PY))
    greet(31 - p, flip)
    greet(31 - p, flip_row)
    greet(far_from, flip)
    greet(far_from, flip_row)
    pl.semaphore_wait(barrier, (PX - 1) + (PY - 1) + 8)

    def scatter(source, lands, group):
        copies = []
        for n, (a, b) in enumerate(AROUND):
            copy = push(
                box(source, CUT_X[a], CUT_Y[b]), lands[n], halo_send.at[group, n], halo_recv.at[group, n],
                wrap(p + a - 1, PX), wrap(q + b - 1, PY),
            )
            copy.start()
            copies.append(copy)
        return copies

    def collect(source, lands, copies, total):
        total[...] = box(source, CUT_X[1], CUT_Y[1])[...]
        for n, (a, b) in enumerate(AROUND):
            copies[n].wait_recv()
            part = box(total, LAND_X[a], LAND_Y[b])
            part[...] = part[...] + lands[n][...]

    def spread(source, window, group):
        copies = []
        for n, (a, b) in enumerate(AROUND):
            copy = push(
                box(source, TAKE_X[a], TAKE_Y[b]), box(window, GIVE_X[a], GIVE_Y[b]),
                halo_send.at[group, n], halo_recv.at[group, n], wrap(p + a - 1, PX), wrap(q + b - 1, PY),
            )
            copy.start()
            copies.append(copy)
        box(window, CUT_X[1], CUT_Y[1])[...] = source[...]
        return copies

    pending = []
    first = scatter(field, land_e, 0)
    pending += first

    greens = [
        push(green.at[3], near, green_send.at[0], green_recv.at[0], 31 - p, flip),
        push(green.at[2 * upper_half], far, green_send.at[1], green_recv.at[1], far_to, flip),
        push(green.at[3, pl.ds(0, 8)], near_row, green_send.at[2], green_recv.at[2], 31 - p, flip_row),
        push(green.at[2 * upper_half, pl.ds(0, 8)], far_row, green_send.at[3], green_recv.at[3], far_to, flip_row),
    ]
    for copy in greens:
        copy.start()
    pending += greens

    def extra_copy(a, b):
        return push(green.at[0], extra, green_send.at[4], green_recv.at[4], a, b)

    def extra_row_copy():
        return push(green.at[0, pl.ds(0, 8)], extra_row, green_send.at[5], green_recv.at[5], SPECIAL, flip_row)

    sends_extra = ((p == 0) | (p == SPECIAL)) & (q < 4)
    sends_row = (p == SPECIAL) & (q > 0) & (q < 4)
    extra_to = q + (p // SPECIAL) * (flip - q)

    @pl.when(sends_extra)
    def _():
        extra_copy(SPECIAL, extra_to).start()

    @pl.when(sends_row)
    def _():
        extra_row_copy().start()

    fine_c, fine_s = fine[0], fine[1]

    def table_body(k, unused):
        coarse_c, coarse_s = coarse[0, pl.ds(k, 1), :], coarse[1, pl.ds(k, 1), :]
        rows = pl.ds(pl.multiple_of(32 * k, 32), 32)
        cos_h[rows, :], cos_l[rows, :] = split(coarse_c * fine_c - coarse_s * fine_s)
        sin_h[rows, :], sin_l[rows, :] = split(coarse_s * fine_c + coarse_c * fine_s)
        return unused

    lax.fori_loop(0, NX // 32, table_body, 0)

    collect(field, land_e, first, grid)

    keep = low_lanes((PX, 128))
    nt = (((1,), (1,)), ((), ()))
    for h in range(2):
        waves = (wave_h[64 * h : 64 * h + 64], wave_l[64 * h : 64 * h + 64])
        for group in range(CX // 4):
            rows = split(grid[4 * group : 4 * group + 4].reshape(256, NZ))
            spectrum = (
                lax.dot_general(waves[0], rows[0], nt, preferred_element_type=F32)
                + lax.dot_general(waves[0], rows[1], nt, preferred_element_type=F32)
                + lax.dot_general(waves[1], rows[0], nt, preferred_element_type=F32)
            )
            for tile in range(2):
                real = spectrum[0:32, 128 * tile : 128 * tile + 128]
                imag = spectrum[32:64, 128 * tile : 128 * tile + 128]
                x = 4 * group + 2 * tile
                s1.at[h][pl.ds(x, PX, stride=24), :] = jnp.where(keep, real, turn(imag))
                s1.at[h][pl.ds(x + 1, PX, stride=24), :] = jnp.where(keep, turn(real), imag)

        @pl.loop(1, PX)
        def _(j):
            to = (p + j) % PX
            rows = pl.ds(pl.multiple_of(24 * to, 8), 24)
            here = pl.ds(pl.multiple_of(24 * p, 8), 24)
            push(s1.at[h, rows], r1.at[h, here], px_send.at[0, h], px_recv.at[0, h], to, q).start()

        here = pl.ds(pl.multiple_of(24 * p, 8), 24)
        r1[h, here, :] = s1[h, here, :]

    second = scatter(cover, land_o, 1)
    pending += second

    keep = low_lanes((KX, 128))
    special = p == SPECIAL
    most = 31 * 24
    for h in range(2):
        drain(r1.at[h, pl.ds(0, most)], px_recv.at[0, h])
        high, low = split(r1[h])
        both_parts = jnp.concatenate([high, low], axis=1)
        one_h[...] = both_parts

        def rows_body(k, unused):
            rows = pl.ds(pl.multiple_of(KX * k, KX), KX)
            data = one_h[...]
            cosine = dot(cos_h[rows, :], data)
            cosine = cosine[:, :128] + cosine[:, 128:] + dot(cos_l[rows, :], data[:, :128])
            sine = dot(sin_h[rows, :], data)
            sine = sine[:, :128] + sine[:, 128:] + dot(sin_l[rows, :], data[:, :128])
            turned = turn(sine)
            value = jnp.where(keep, cosine + turned, cosine - turned)
            if h == 1:
                below = jnp.where(keep, cosine, -turned)
                above = jnp.where(keep, turn(cosine), -sine)
                parted = jnp.where(k < 4, below, above)
                top = (lax.broadcasted_iota(jnp.int32, (KX, 128), 0) == 0) & (k % 4 == 0)
                value = jnp.where(special & jnp.logical_not(top), parted, jnp.where(special, cosine, value))
            y1[h, k] = value

            @pl.when(k != q)
            def _():
                push(y1.at[h, k], t1.at[h, q], py_send.at[0, h], py_recv.at[0, h], p, k).start()

            return unused

        lax.fori_loop(0, PY, rows_body, 0)
        t1[h, q] = y1[h, q]

    for copy in greens:
        copy.wait_recv()

    @pl.when(p == SPECIAL)
    def _():
        extra_copy(SPECIAL, extra_to).wait_recv()

    @pl.when((p == SPECIAL) & (q > 4))
    def _():
        extra_row_copy().wait_recv()

    flips = row_flip[...]
    lanes_flip = lane_flip[...]

    def permute(value):
        high, low = split(value)
        return dot(high, lanes_flip) + dot(low, lanes_flip)

    def mirror(plane, row):
        high, low = split(plane)
        turned = dot(flips, high) + dot(flips, low)
        top = lax.broadcasted_iota(jnp.int32, turned.shape, 0) == 0
        return permute(jnp.where(top, jnp.broadcast_to(row, turned.shape), turned))

    upper = special & (q >= 4)
    lower = special & (q < 4)
    gs[0] = 0.5 * (green[1] + mirror(near[...], near_row[0:1]))
    base = jnp.where(p < 16, green[2], jnp.where(lower, extra[...], green[0]))
    plane = jnp.where(upper, extra[...], far[...])
    row = jnp.where(upper, extra_row[0:1], far_row[0:1])
    half = 0.5 * (base + mirror(plane, row))
    packed_rows = jnp.concatenate(
        [jnp.broadcast_to(far_row[0:1], (8, NY)), jnp.broadcast_to(green[0, 0:1], (8, NY))], axis=0
    )
    packed_rows = 0.5 * (packed_rows + permute(packed_rows))
    packed = special & (q % 4 == 0)
    top = (lax.broadcasted_iota(jnp.int32, (KX, NY), 0) == 0) & packed
    gs[1] = jnp.where(top, jnp.broadcast_to(packed_rows[0:1], (KX, NY)), half)
    gx[...] = packed_rows[8:16]

    tables = (table_h[...], table_l[...])
    for h in range(2):
        drain(t1.at[h, pl.ds(0, PY - 1)], py_recv.at[0, h])
        for tile in range(4):
            even, odd = t1[h, 2 * tile], t1[h, 2 * tile + 1]
            lanes = slice(128 * tile, 128 * tile + 128)
            work_h[0:96, lanes], work_l[0:96, lanes] = split(jnp.where(keep, even, turn(odd)))
            work_h[96:192, lanes], work_l[96:192, lanes] = split(jnp.where(keep, turn(even), odd))
        wave = dot3((work_h[0:192], work_l[0:192]), tables)
        re_c, re_s = wave[0:96, :NY], wave[0:96, NY:]
        im_c, im_s = wave[96:192, :NY], wave[96:192, NY:]
        real, imag = re_c + im_s, im_c - re_s
        if h == 1:
            real, imag = jnp.where(top, re_c, real), jnp.where(top, -re_s, imag)
            fix = gx[...]
            work_h[192:200], work_l[192:200] = split(fix * im_c[0:8])
            work_h[200:208], work_l[200:208] = split(fix * -im_s[0:8])
        work_h[0:96], work_l[0:96] = split(gs[h] * real)
        work_h[96:192], work_l[96:192] = split(gs[h] * imag)
        used = slice(0, 208 if h == 1 else 192)
        wave = dot3((work_h[used], work_l[used]), tables)
        real = wave[0:96, :NY] - wave[96:192, NY:]
        imag = wave[96:192, :NY] + wave[0:96, NY:]
        if h == 1:
            fix = wave[192:200, :NY] - wave[200:208, NY:]
            imag = jnp.where(top, jnp.broadcast_to(fix[0:1], (KX, NY)), imag)
        for tile in range(4):
            lanes = slice(128 * tile, 128 * tile + 128)
            re, im = real[:, lanes], imag[:, lanes]
            y2[h, 2 * tile] = jnp.where(keep, re, turn(im))
            y2[h, 2 * tile + 1] = jnp.where(keep, turn(re), im)

        @pl.loop(1, PY)
        def _(j):
            to = (q + j) % PY
            push(y2.at[h, to], t2.at[h, q], py_send.at[1, h], py_recv.at[1, h], p, to).start()

        t2[h, q] = y2[h, q]

    collect(cover, land_o, second, occupancy)
    third = spread(occupancy, oc_window, 2)
    pending += third

    for h in range(2):
        drain(t2.at[h, pl.ds(0, PY - 1)], py_recv.at[1, h])
        for k in range(PY):
            value = t2[h, k]
            turned = turn(value)
            one = value
            two = jnp.where(keep, -turned, turned)
            if h == 1:
                if k < 4:
                    one_s, two_s = jnp.where(keep, 2.0 * value, 0.0), jnp.where(keep, -2.0 * turned, 0.0)
                else:
                    one_s, two_s = jnp.where(keep, 0.0, 2.0 * turned), jnp.where(keep, 0.0, -2.0 * value)
                if k % 4 == 0:
                    row_zero = lax.broadcasted_iota(jnp.int32, (KX, 128), 0) == 0
                    one_s, two_s = jnp.where(row_zero, value, one_s), jnp.where(row_zero, 0.0, two_s)
                one, two = jnp.where(special, one_s, one), jnp.where(special, two_s, two)
            rows = slice(KX * k, KX * k + KX)
            one_h[rows, 0:128], one_h[rows, 128:256] = split(one)
            two_h[rows, 0:128], two_h[rows, 128:256] = split(two)

        def unrows_body(k, unused):
            rows = pl.ds(pl.multiple_of(KX * k, KX), KX)
            one, two = one_h[...], two_h[...]
            result = dot(cos_h[rows, :], one) + dot(sin_h[rows, :], two)
            result = result[:, :128] + result[:, 128:] + dot(cos_l[rows, :], one[:, :128]) + dot(sin_l[rows, :], two[:, :128])
            s2[h, rows, :] = result
            for i in range(4):
                to = 4 * k + i

                @pl.when(to != p)
                def _():
                    part = pl.ds(pl.multiple_of(24 * to, 8), 24)
                    here = pl.ds(pl.multiple_of(24 * p, 8), 24)
                    push(s2.at[h, part], r2.at[h, here], px_send.at[1, h], px_recv.at[1, h], to, q).start()

            return unused

        lax.fori_loop(0, 8, unrows_body, 0)
        here = pl.ds(pl.multiple_of(24 * p, 8), 24)
        r2[h, here, :] = s2[h, here, :]

    keep = low_lanes((PX, 128))
    for h in range(2):
        drain(r2.at[h, pl.ds(0, most)], px_recv.at[1, h])
        waves = (back_h[64 * h : 64 * h + 64], back_l[64 * h : 64 * h + 64])
        for tile in range(CX // 2):
            x = 2 * tile
            even = r2.at[h][pl.ds(x, PX, stride=24), :]
            odd = r2.at[h][pl.ds(x + 1, PX, stride=24), :]
            parts = [jnp.where(keep, even, turn(odd)), jnp.where(keep, turn(even), odd)]
            block = split(jnp.concatenate(parts, axis=0).T)
            value = dot3(block, waves).reshape(2, CY, NZ)
            if h == 0:
                potential[x : x + 2] = value
            else:
                potential[x : x + 2] = potential[x : x + 2] + value

    fourth = spread(potential, mu_window, 3)
    pending += fourth
    for copy in third + fourth:
        copy.wait_recv()

    for copy in pending:
        copy.wait_send()

    @pl.when(sends_extra)
    def _():
        extra_copy(SPECIAL, extra_to).wait_send()

    @pl.when(sends_row)
    def _():
        extra_row_copy().wait_send()

    for h in range(2):
        drain(s1.at[h, pl.ds(0, most)], px_send.at[0, h])
        drain(s2.at[h, pl.ds(0, most)], px_send.at[1, h])
        drain(y1.at[h, pl.ds(0, PY - 1)], py_send.at[0, h])
        drain(y2.at[h, pl.ds(0, PY - 1)], py_send.at[1, h])


def update_kernel(start, ids, misfit, eta, field, cover, out, potential):
    potential[...] = field[:CX, :CY]
    sublane = lax.broadcasted_iota(jnp.int32, (32, NZ), 0)
    for b in range(eta.shape[0]):
        weight = misfit[ids[b]]
        sx = start[0, b]
        sy = pl.multiple_of(start[1, b], 8)

        def body(i, unused):
            value = eta[b, i]
            before = jnp.where(i > 0, eta[b, jnp.maximum(i - 1, 0)], 0.0)
            after = jnp.where(i < 31, eta[b, jnp.minimum(i + 1, 31)], 0.0)
            above = jnp.where(sublane == 0, 0.0, pltpu.roll(value, 1, axis=0))
            below = jnp.where(sublane == 31, 0.0, pltpu.roll(value, 31, axis=0))
            lap = before + after + above + below + pltpu.roll(value, 1, axis=1) + pltpu.roll(value, 127, axis=1) - 6.0 * value
            mu = field[sx + i, pl.ds(sy, 32), :]
            total = cover[sx + i, pl.ds(sy, 32), :]
            square = value * value
            force = value * square - value + 2.0 * COUPLING * value * (total - square)
            force = force - GRADIENT * lap + 2.0 * weight * value * mu
            out[b, i] = value - RATE * force
            return unused

        lax.fori_loop(0, 32, body, 0, unroll=2)


def on_device(eta, corners, grain_ids, misfit, green):
    p, q = lax.axis_index("px"), lax.axis_index("py")
    start = jnp.stack([corners[:, 0] * STEP - p * CX, corners[:, 1] * STEP - q * CY]).astype(jnp.int32)
    forward, inverse = depth_tables()
    coarse, fine = wave_rows(24, 32, NX), wave_rows(32, 1, NX)
    patch = shaped(CX + OV, CY + OV, NZ)
    field, cover = call(place_kernel, [patch, patch], [SM, SM, SM, VM], (start, grain_ids, misfit, eta))

    def lands():
        return [
            pltpu.VMEM((CUT_X[a][1] - CUT_X[a][0], CUT_Y[b][1] - CUT_Y[b][0], NZ), F32) for a, b in AROUND
        ]

    dma = pltpu.SemaphoreType.DMA
    scratch = [
        pltpu.VMEM((CX, CY, NZ), F32),
        pltpu.VMEM((2, NX, 128), F32),
        pltpu.VMEM((2, NX, 128), F32),
        *[pltpu.VMEM((2, PY, KX, 128), F32)] * 4,
        pltpu.VMEM((2, NX, 128), F32),
        pltpu.VMEM((2, NX, 128), F32),
        *[pltpu.VMEM((NX, NX), BF16)] * 4,
        *[pltpu.VMEM((KX, NY), F32)] * 3,
        *[pltpu.VMEM((8, NY), F32)] * 3,
        pltpu.VMEM((2, KX, NY), F32),
        pltpu.VMEM((8, NY), F32),
        *[pltpu.VMEM((208, NY), BF16)] * 2,
        *[pltpu.VMEM((NX, 256), BF16)] * 2,
        pltpu.VMEM((CX, CY, NZ), F32),
        pltpu.VMEM((CX, CY, NZ), F32),
        lands(),
        lands(),
        dma((4, 8)),
        dma((4, 8)),
        dma((6,)),
        dma((6,)),
        *[dma((2, 2))] * 4,
    ]
    mu, total = call(
        mega_kernel,
        [patch, patch],
        [VM] * 13,
        (field, cover, green, coarse, fine, *halves(forward), *halves(inverse), *column_tables(), *mirror_tables()),
        scratch=scratch,
        collective_id=0,
        has_side_effects=True,
    )
    eta_next, potential = call(
        update_kernel,
        [shaped(*eta.shape), shaped(CX, CY, NZ)],
        [SM] * 3 + [VM] * 3,
        (start, grain_ids, misfit, eta, mu, total),
    )
    return eta_next, potential


def solution(mesh):
    in_specs = (P(("px", "py"), None, None, None), P(("px", "py"), None), P(("px", "py")), P(), P("px", "py", None))
    out_specs = (P(("px", "py"), None, None, None), P("px", "py", None))
    return jax.shard_map(on_device, mesh=mesh, in_specs=in_specs, out_specs=out_specs, check_vma=False)
```

```python
import functools

import jax
import jax.numpy as jnp
import numpy as np
from jax import lax
from jax.experimental import pallas as pl
from jax.experimental.pallas import tpu as pltpu
from jax.sharding import PartitionSpec as P

NX, NY, NZ = 768, 512, 128
STEP = 8
PX, PY = 32, 8
CX, CY = NX // PX, NY // PY
OV = 24
KX = NX // PY
F32 = jnp.float32
BF16 = jnp.bfloat16
SPECIAL = 16
RATE = 0.2
GRADIENT = 0.1
COUPLING = 1.5

SM = pl.BlockSpec(memory_space=pltpu.SMEM)


def halves(array):
    high = np.asarray(array, np.float32).astype(jnp.bfloat16)
    low = (np.asarray(array, np.float64) - high.astype(np.float64)).astype(jnp.bfloat16)
    return high, low


def slot_wave(p, h):
    if h == 0:
        return 4 * p + 1
    return 4 * p + 2 if p < 16 else 4 * p


def depth_tables():
    z = np.arange(NZ)
    forward = np.zeros((NZ, NZ))
    inverse = np.zeros((NZ, NZ))
    total = NX * NY * NZ
    for h in range(2):
        for p in range(PX):
            row_re, row_im = h * 64 + p, h * 64 + 32 + p
            wave = slot_wave(p, h)
            cosine = np.cos(2 * np.pi * ((wave * z) % NZ) / NZ)
            sine = np.sin(2 * np.pi * ((wave * z) % NZ) / NZ)
            if p == SPECIAL and h == 1:
                forward[row_re], forward[row_im] = 1.0, (-1.0) ** z
                inverse[row_re], inverse[row_im] = 1.0 / total, (-1.0) ** z / total
            else:
                forward[row_re], forward[row_im] = cosine, -sine
                inverse[row_re], inverse[row_im] = 2 * cosine / total, -2 * sine / total
    return forward, inverse


def wave_rows(count, step, length):
    angle = 2 * np.pi * ((step * np.arange(count)[:, None] * np.arange(length)[None]) % length) / length
    return np.stack([np.cos(angle), np.sin(angle)]).astype(np.float32)


def column_tables():
    k = np.arange(NY)
    angle = 2 * np.pi * ((k[:, None] * k[None]) % NY) / NY
    return halves(np.concatenate([np.cos(angle), np.sin(angle)], axis=1))


def mirror_tables():
    rows = np.zeros((KX, KX), np.float32)
    for j in range(1, KX):
        rows[j, KX - j] = 1.0
    lanes = np.zeros((NY, NY), np.float32)
    for k in range(NY):
        lanes[(NY - k) % NY, k] = 1.0
    return rows.astype(jnp.bfloat16), lanes.astype(jnp.bfloat16)


def split(value):
    high = value.astype(BF16)
    return high, (value - high.astype(F32)).astype(BF16)


def dot(a, b):
    return jnp.dot(a, b, preferred_element_type=F32)


def dot3(a, b):
    return dot(a[0], b[0]) + dot(a[0], b[1]) + dot(a[1], b[0])


def turn(value):
    return pltpu.roll(value, 64, axis=value.ndim - 1)


def low_lanes(shape):
    return lax.broadcasted_iota(jnp.int32, shape, len(shape) - 1) < 64


def shaped(*shape, dtype=F32):
    return jax.ShapeDtypeStruct(shape, dtype)


MESH = pl.DeviceIdType.MESH
CUT_X = ((0, 12), (12, 36), (36, 48))
CUT_Y = ((0, 8), (8, 72), (72, 88))
TAKE_X = ((0, 12), (0, 24), (12, 24))
TAKE_Y = ((0, 16), (0, 64), (56, 64))
GIVE_X = ((36, 48), (12, 36), (0, 12))
GIVE_Y = ((72, 88), (8, 72), (0, 8))
AROUND = [(a, b) for a, b in ((0, 1), (2, 1), (1, 0), (1, 2), (0, 0), (0, 2), (2, 0), (2, 2))]


def box(ref, x, y):
    return ref.at[pl.ds(x[0], x[1] - x[0]), pl.ds(y[0], y[1] - y[0])]


def wrap(value, count):
    return (value + count) % count


def push(source, target, send, receive, p, q):
    return pltpu.make_async_remote_copy(
        src_ref=source, dst_ref=target, send_sem=send, recv_sem=receive, device_id=(p, q), device_id_type=MESH
    )


def drain(ref, semaphore):
    pltpu.make_async_copy(ref, ref, semaphore).wait()


def mega_kernel(
    eta_in, field_in, cover_in, green_in, coarse_in, fine_in, wave_h_in, wave_l_in, back_h_in, back_l_in,
    table_h_in, table_l_in, row_flip_in, lane_flip_in,
    base_out, mu_out, oc_out,
    green, coarse, fine, wave_h, wave_l, back_h, back_l, table_h, table_l, row_flip, lane_flip,
    load_sem, eta_sem, out_sem, eta, result, field, cover, mu_window, oc_window,
    grid, s1, r1, y1, t1, y2, t2, s2, r2, cos_h, cos_l, sin_h, sin_l,
    near, far, extra, near_row, far_row, extra_row, gs, gx, work_h, work_l, one_h, two_h, potential,
    low_y, high_y, low_x, high_x, side_o, low_o, high_o, halo_send, halo_recv, green_send, green_recv, px_send, px_recv, py_send, py_recv,
):
    p, q = lax.axis_index("px"), lax.axis_index("py")
    upper_half = p // 16
    far_to = 31 - p + (1 - upper_half) - 16 * (1 - (p + 31) // 32)
    far_from = 31 - p + upper_half - 16 * upper_half * (1 - (p + 15) // 32)
    flip, flip_row = 7 - q, (8 - q) % 8

    pairs = (
        (green_in, green), (coarse_in, coarse), (fine_in, fine), (wave_h_in, wave_h), (wave_l_in, wave_l),
        (back_h_in, back_h), (back_l_in, back_l), (table_h_in, table_h), (table_l_in, table_l),
        (row_flip_in, row_flip), (lane_flip_in, lane_flip),
    )
    boxes = eta_in.shape[0]
    patches = [
        pltpu.make_async_copy(field_in, field, eta_sem.at[0]),
        pltpu.make_async_copy(cover_in, cover, eta_sem.at[1]),
        pltpu.make_async_copy(eta_in, eta, eta_sem.at[2]),
    ]
    loads = [pltpu.make_async_copy(source, target, load_sem.at[n]) for n, (source, target) in enumerate(pairs)]
    for copy in patches + loads:
        copy.start()

    barrier = pltpu.get_barrier_semaphore()

    def greet(a, b):
        pl.semaphore_signal(barrier, inc=1, device_id=(a, b), device_id_type=MESH)

    @pl.loop(1, PX)
    def _(j):
        greet((p + j) % PX, q)

    @pl.loop(1, PY)
    def _(j):
        greet(p, (q + j) % PY)

    for a in (-1, 1):
        for b in (-1, 1):
            greet(wrap(p + a, PX), wrap(q + b, PY))
    greet(31 - p, flip)
    greet(31 - p, flip_row)
    greet(far_from, flip)
    greet(far_from, flip_row)
    pl.semaphore_wait(barrier, (PX - 1) + (PY - 1) + 8)

    def spread(source, window, group):
        copies = []
        for n, (a, b) in enumerate(AROUND):
            copy = push(
                box(source, TAKE_X[a], TAKE_Y[b]), box(window, GIVE_X[a], GIVE_Y[b]),
                halo_send.at[group, n], halo_recv.at[group, n], wrap(p + a - 1, PX), wrap(q + b - 1, PY),
            )
            copy.start()
            copies.append(copy)
        box(window, CUT_X[1], CUT_Y[1])[...] = source[...]
        return copies

    near_copies = [
        push(green_in.at[3], near, green_send.at[0], green_recv.at[0], 31 - p, flip),
        push(green_in.at[3, pl.ds(0, 8)], near_row, green_send.at[2], green_recv.at[2], 31 - p, flip_row),
    ]
    far_copies = [
        push(green_in.at[2 * upper_half], far, green_send.at[1], green_recv.at[1], far_to, flip),
        push(green_in.at[2 * upper_half, pl.ds(0, 8)], far_row, green_send.at[3], green_recv.at[3], far_to, flip_row),
    ]
    for copy in near_copies:
        copy.start()
    pending = near_copies + far_copies
    next_p, last_p, next_q, last_q = wrap(p + 1, PX), wrap(p - 1, PX), wrap(q + 1, PY), wrap(q - 1, PY)

    def halo(source, target, slot, a, b):
        copy = push(source, target, halo_send.at[0, slot], halo_recv.at[0, slot], a, b)
        pending.append(copy)
        return copy

    patches[0].wait()
    along_y = [
        halo(field.at[:, pl.ds(0, 8)], low_y, 0, p, last_q),
        halo(field.at[:, pl.ds(72, 16)], high_y, 1, p, next_q),
    ]
    for copy in along_y:
        copy.start()
    patches[1].wait()
    side_copy = halo(cover.at[:, pl.ds(CY, OV)], side_o, 2, p, next_q)
    side_copy.start()
    for copy in along_y:
        copy.wait_recv()
    field[:, 64:72] = field[:, 64:72] + low_y[...]
    field[:, 8:24] = field[:, 8:24] + high_y[...]
    along_x = [
        halo(field.at[pl.ds(0, 12), pl.ds(8, CY)], low_x, 3, last_p, q),
        halo(field.at[pl.ds(36, 12), pl.ds(8, CY)], high_x, 4, next_p, q),
    ]
    for copy in along_x:
        copy.start()

    def extra_copy(a, b):
        return push(green_in.at[0], extra, green_send.at[4], green_recv.at[4], a, b)

    def extra_row_copy():
        return push(green_in.at[0, pl.ds(0, 8)], extra_row, green_send.at[5], green_recv.at[5], SPECIAL, flip_row)

    sends_extra = ((p == 0) | (p == SPECIAL)) & (q < 4)
    sends_row = (p == SPECIAL) & (q > 0) & (q < 4)
    extra_to = q + (p // SPECIAL) * (flip - q)

    for copy in loads:
        copy.wait()
    fine_c, fine_s = fine[0], fine[1]

    def table_body(k, unused):
        coarse_c, coarse_s = coarse[0, pl.ds(k, 1), :], coarse[1, pl.ds(k, 1), :]
        rows = pl.ds(pl.multiple_of(32 * k, 32), 32)
        cos_h[rows, :], cos_l[rows, :] = split(coarse_c * fine_c - coarse_s * fine_s)
        sin_h[rows, :], sin_l[rows, :] = split(coarse_s * fine_c + coarse_c * fine_s)
        return unused

    lax.fori_loop(0, NX // 32, table_body, 0)

    for copy in along_x:
        copy.wait_recv()
    grid[0:12] = field[12:24, 8:72] + high_x[...]
    grid[12:24] = field[24:36, 8:72] + low_x[...]

    keep = low_lanes((PX, 128))
    nt = (((1,), (1,)), ((), ()))
    for h in range(2):
        waves = (wave_h[64 * h : 64 * h + 64], wave_l[64 * h : 64 * h + 64])
        for group in range(CX // 4):
            rows = split(grid[4 * group : 4 * group + 4].reshape(256, NZ))
            spectrum = (
                lax.dot_general(waves[0], rows[0], nt, preferred_element_type=F32)
                + lax.dot_general(waves[0], rows[1], nt, preferred_element_type=F32)
                + lax.dot_general(waves[1], rows[0], nt, preferred_element_type=F32)
            )
            for tile in range(2):
                real = spectrum[0:32, 128 * tile : 128 * tile + 128]
                imag = spectrum[32:64, 128 * tile : 128 * tile + 128]
                x = 4 * group + 2 * tile
                s1.at[h][pl.ds(x, PX, stride=24), :] = jnp.where(keep, real, turn(imag))
                s1.at[h][pl.ds(x + 1, PX, stride=24), :] = jnp.where(keep, turn(real), imag)

        @pl.loop(1, PX)
        def _(j):
            to = (p + j) % PX
            rows = pl.ds(pl.multiple_of(24 * to, 8), 24)
            here = pl.ds(pl.multiple_of(24 * p, 8), 24)
            push(s1.at[h, rows], r1.at[h, here], px_send.at[0, h], px_recv.at[0, h], to, q).start()

        here = pl.ds(pl.multiple_of(24 * p, 8), 24)
        r1[h, here, :] = s1[h, here, :]

    for copy in far_copies:
        copy.start()

    @pl.when(sends_extra)
    def _():
        extra_copy(SPECIAL, extra_to).start()

    @pl.when(sends_row)
    def _():
        extra_row_copy().start()

    side_copy.wait_recv()
    cover[:, 0:OV] = cover[:, 0:OV] + side_o[...]
    cover_x = [
        halo(cover.at[pl.ds(0, 24), pl.ds(0, CY)], low_o, 5, last_p, q),
        halo(cover.at[pl.ds(24, 24), pl.ds(0, CY)], high_o, 6, next_p, q),
    ]
    for copy in cover_x:
        copy.start()

    flips = row_flip[...]
    lanes_flip = lane_flip[...]

    def permute(value):
        high, low = split(value)
        return dot(high, lanes_flip) + dot(low, lanes_flip)

    def mirror(plane, row):
        high, low = split(plane)
        turned = dot(flips, high) + dot(flips, low)
        first_row = lax.broadcasted_iota(jnp.int32, turned.shape, 0) == 0
        return permute(jnp.where(first_row, jnp.broadcast_to(row, turned.shape), turned))

    for copy in near_copies:
        copy.wait_recv()
    gs[0] = 0.5 * (green[1] + mirror(near[...], near_row[0:1]))

    keep = low_lanes((KX, 128))
    special = p == SPECIAL
    most = 31 * 24
    for h in range(2):
        drain(r1.at[h, pl.ds(0, most)], px_recv.at[0, h])
        high, low = split(r1[h])
        both_parts = jnp.concatenate([high, low], axis=1)
        one_h[...] = both_parts

        def rows_body(k, unused):
            rows = pl.ds(pl.multiple_of(KX * k, KX), KX)
            data = one_h[...]
            cosine = dot(cos_h[rows, :], data)
            cosine = cosine[:, :128] + cosine[:, 128:] + dot(cos_l[rows, :], data[:, :128])
            sine = dot(sin_h[rows, :], data)
            sine = sine[:, :128] + sine[:, 128:] + dot(sin_l[rows, :], data[:, :128])
            turned = turn(sine)
            value = jnp.where(keep, cosine + turned, cosine - turned)
            if h == 1:
                below = jnp.where(keep, cosine, -turned)
                above = jnp.where(keep, turn(cosine), -sine)
                parted = jnp.where(k < 4, below, above)
                top = (lax.broadcasted_iota(jnp.int32, (KX, 128), 0) == 0) & (k % 4 == 0)
                value = jnp.where(special & jnp.logical_not(top), parted, jnp.where(special, cosine, value))
            y1[h, k] = value

            @pl.when(k != q)
            def _():
                push(y1.at[h, k], t1.at[h, q], py_send.at[0, h], py_recv.at[0, h], p, k).start()

            return unused

        lax.fori_loop(0, PY, rows_body, 0)
        t1[h, q] = y1[h, q]

    packed = special & (q % 4 == 0)
    top = (lax.broadcasted_iota(jnp.int32, (KX, NY), 0) == 0) & packed

    def second_green():
        for copy in far_copies:
            copy.wait_recv()

        @pl.when(p == SPECIAL)
        def _():
            extra_copy(SPECIAL, extra_to).wait_recv()

        @pl.when((p == SPECIAL) & (q > 4))
        def _():
            extra_row_copy().wait_recv()

        upper = special & (q >= 4)
        lower = special & (q < 4)
        base = jnp.where(p < 16, green[2], jnp.where(lower, extra[...], green[0]))
        plane = jnp.where(upper, extra[...], far[...])
        row = jnp.where(upper, extra_row[0:1], far_row[0:1])
        half = 0.5 * (base + mirror(plane, row))
        packed_rows = jnp.concatenate(
            [jnp.broadcast_to(far_row[0:1], (8, NY)), jnp.broadcast_to(green[0, 0:1], (8, NY))], axis=0
        )
        packed_rows = 0.5 * (packed_rows + permute(packed_rows))
        gs[1] = jnp.where(top, jnp.broadcast_to(packed_rows[0:1], (KX, NY)), half)
        gx[...] = packed_rows[8:16]

    tables = (table_h[...], table_l[...])
    for h in range(2):
        if h == 1:
            second_green()
        drain(t1.at[h, pl.ds(0, PY - 1)], py_recv.at[0, h])
        for tile in range(4):
            even, odd = t1[h, 2 * tile], t1[h, 2 * tile + 1]
            lanes = slice(128 * tile, 128 * tile + 128)
            work_h[0:96, lanes], work_l[0:96, lanes] = split(jnp.where(keep, even, turn(odd)))
            work_h[96:192, lanes], work_l[96:192, lanes] = split(jnp.where(keep, turn(even), odd))
        wave = dot3((work_h[0:192], work_l[0:192]), tables)
        re_c, re_s = wave[0:96, :NY], wave[0:96, NY:]
        im_c, im_s = wave[96:192, :NY], wave[96:192, NY:]
        real, imag = re_c + im_s, im_c - re_s
        if h == 1:
            real, imag = jnp.where(top, re_c, real), jnp.where(top, -re_s, imag)
            fix = gx[...]
            work_h[192:200], work_l[192:200] = split(fix * im_c[0:8])
            work_h[200:208], work_l[200:208] = split(fix * -im_s[0:8])
        work_h[0:96], work_l[0:96] = split(gs[h] * real)
        work_h[96:192], work_l[96:192] = split(gs[h] * imag)
        used = slice(0, 208 if h == 1 else 192)
        wave = dot3((work_h[used], work_l[used]), tables)
        real = wave[0:96, :NY] - wave[96:192, NY:]
        imag = wave[96:192, :NY] + wave[0:96, NY:]
        if h == 1:
            fix = wave[192:200, :NY] - wave[200:208, NY:]
            imag = jnp.where(top, jnp.broadcast_to(fix[0:1], (KX, NY)), imag)
        for tile in range(4):
            lanes = slice(128 * tile, 128 * tile + 128)
            re, im = real[:, lanes], imag[:, lanes]
            y2[h, 2 * tile] = jnp.where(keep, re, turn(im))
            y2[h, 2 * tile + 1] = jnp.where(keep, turn(re), im)

        @pl.loop(1, PY)
        def _(j):
            to = (q + j) % PY
            push(y2.at[h, to], t2.at[h, q], py_send.at[1, h], py_recv.at[1, h], p, to).start()

        t2[h, q] = y2[h, q]

    for copy in cover_x:
        copy.wait_recv()
    oc_window[0:24, 0:CY] = cover[0:24, 0:CY] + high_o[...]
    oc_window[24:48, 0:CY] = cover[24:48, 0:CY] + low_o[...]
    cover_y = halo(oc_window.at[:, pl.ds(0, OV)], oc_window.at[:, pl.ds(CY, OV)], 7, p, last_q)
    cover_y.start()

    for h in range(2):
        drain(t2.at[h, pl.ds(0, PY - 1)], py_recv.at[1, h])
        for k in range(PY):
            value = t2[h, k]
            turned = turn(value)
            one = value
            two = jnp.where(keep, -turned, turned)
            if h == 1:
                if k < 4:
                    one_s, two_s = jnp.where(keep, 2.0 * value, 0.0), jnp.where(keep, -2.0 * turned, 0.0)
                else:
                    one_s, two_s = jnp.where(keep, 0.0, 2.0 * turned), jnp.where(keep, 0.0, -2.0 * value)
                if k % 4 == 0:
                    row_zero = lax.broadcasted_iota(jnp.int32, (KX, 128), 0) == 0
                    one_s, two_s = jnp.where(row_zero, value, one_s), jnp.where(row_zero, 0.0, two_s)
                one, two = jnp.where(special, one_s, one), jnp.where(special, two_s, two)
            rows = slice(KX * k, KX * k + KX)
            one_h[rows, 0:128], one_h[rows, 128:256] = split(one)
            two_h[rows, 0:128], two_h[rows, 128:256] = split(two)

        def unrows_body(k, unused):
            rows = pl.ds(pl.multiple_of(KX * k, KX), KX)
            one, two = one_h[...], two_h[...]
            result = dot(cos_h[rows, :], one) + dot(sin_h[rows, :], two)
            result = result[:, :128] + result[:, 128:] + dot(cos_l[rows, :], one[:, :128]) + dot(sin_l[rows, :], two[:, :128])
            s2[h, rows, :] = result
            for i in range(4):
                to = 4 * k + i

                @pl.when(to != p)
                def _():
                    part = pl.ds(pl.multiple_of(24 * to, 8), 24)
                    here = pl.ds(pl.multiple_of(24 * p, 8), 24)
                    push(s2.at[h, part], r2.at[h, here], px_send.at[1, h], px_recv.at[1, h], to, q).start()

            return unused

        lax.fori_loop(0, 8, unrows_body, 0)
        here = pl.ds(pl.multiple_of(24 * p, 8), 24)
        r2[h, here, :] = s2[h, here, :]

    cover_y.wait_recv()
    oc_copy = pltpu.make_async_copy(oc_window, oc_out, out_sem.at[boxes])
    oc_copy.start()
    patches[2].wait()
    sublane = lax.broadcasted_iota(jnp.int32, (32, NZ), 0)
    outs = [oc_copy]
    for b in range(boxes):

        def base_body(i, unused):
            value = eta[b, i]
            before = jnp.where(i > 0, eta[b, jnp.maximum(i - 1, 0)], 0.0)
            after = jnp.where(i < 31, eta[b, jnp.minimum(i + 1, 31)], 0.0)
            above = jnp.where(sublane == 0, 0.0, pltpu.roll(value, 1, axis=0))
            below = jnp.where(sublane == 31, 0.0, pltpu.roll(value, 31, axis=0))
            lap = before + after + above + below + pltpu.roll(value, 1, axis=1) + pltpu.roll(value, 127, axis=1)
            lap = lap - 6.0 * value
            square = value * value
            force = value * square - value - 2.0 * COUPLING * value * square - GRADIENT * lap
            result[b, i] = value - RATE * force
            return unused

        lax.fori_loop(0, 32, base_body, 0, unroll=2)
        outs.append(pltpu.make_async_copy(result.at[b], base_out.at[b], out_sem.at[b]))
        outs[-1].start()

    keep = low_lanes((PX, 128))
    for h in range(2):
        drain(r2.at[h, pl.ds(0, most)], px_recv.at[1, h])
        waves = (back_h[64 * h : 64 * h + 64], back_l[64 * h : 64 * h + 64])
        for tile in range(CX // 2):
            x = 2 * tile
            even = r2.at[h][pl.ds(x, PX, stride=24), :]
            odd = r2.at[h][pl.ds(x + 1, PX, stride=24), :]
            parts = [jnp.where(keep, even, turn(odd)), jnp.where(keep, turn(even), odd)]
            block = split(jnp.concatenate(parts, axis=0).T)
            value = dot3(block, waves).reshape(2, CY, NZ)
            if h == 0:
                potential[x : x + 2] = value
            else:
                potential[x : x + 2] = potential[x : x + 2] + value

    around = spread(potential, mu_window, 1)
    pending += around
    for copy in around:
        copy.wait_recv()
    outs.append(pltpu.make_async_copy(mu_window, mu_out, out_sem.at[boxes + 1]))
    outs[-1].start()

    for copy in pending:
        copy.wait_send()

    @pl.when(sends_extra)
    def _():
        extra_copy(SPECIAL, extra_to).wait_send()

    @pl.when(sends_row)
    def _():
        extra_row_copy().wait_send()

    for h in range(2):
        drain(s1.at[h, pl.ds(0, most)], px_send.at[0, h])
        drain(s2.at[h, pl.ds(0, most)], px_send.at[1, h])
        drain(y1.at[h, pl.ds(0, PY - 1)], py_send.at[0, h])
        drain(y2.at[h, pl.ds(0, PY - 1)], py_send.at[1, h])
    for copy in outs:
        copy.wait()


def place_kernel(corners, ids, misfit, eta, field, cover):
    shift_x, shift_y = lax.axis_index("px") * CX, lax.axis_index("py") * CY
    field[...] = jnp.zeros_like(field)
    cover[...] = jnp.zeros_like(cover)
    for b in range(eta.shape[0]):
        weight = misfit[ids[b]]
        sx = corners[b, 0] * STEP - shift_x
        sy = pl.multiple_of(corners[b, 1] * STEP - shift_y, 8)

        def body(i, unused):
            value = eta[b, i]
            square = value * value
            rows = pl.ds(sy, 32)
            field[sx + i, rows, :] = field[sx + i, rows, :] + weight * square
            cover[sx + i, rows, :] = cover[sx + i, rows, :] + square
            return unused

        lax.fori_loop(0, 32, body, 0, unroll=4)


def final_kernel(corners, ids, misfit, eta, base, mu_window, oc_window, out, potential):
    b = pl.program_id(0)
    shift_x, shift_y = lax.axis_index("px") * CX, lax.axis_index("py") * CY

    @pl.when(b == 0)
    def _():
        potential[...] = mu_window[:CX, :CY]

    factor = 2.0 * RATE * misfit[ids[b]]
    sx = corners[b, 0] * STEP - shift_x
    sy = pl.multiple_of(corners[b, 1] * STEP - shift_y, 8)

    def body(i, unused):
        rows = pl.ds(sy, 32)
        mu = mu_window[sx + i, rows, :]
        total = oc_window[sx + i, rows, :]
        out[0, i] = base[0, i] - eta[0, i] * (2.0 * RATE * COUPLING * total + factor * mu)
        return unused

    lax.fori_loop(0, 32, body, 0, unroll=4)


def on_device(eta, corners, grain_ids, misfit, green):
    forward, inverse = depth_tables()
    patch = pltpu.VMEM((CX + OV, CY + OV, NZ), F32)
    dma = pltpu.SemaphoreType.DMA
    arrays = [
        green, wave_rows(24, 32, NX), wave_rows(32, 1, NX), *halves(forward), *halves(inverse), *column_tables(),
        *mirror_tables(),
    ]
    boxes = eta.shape[0]
    cells = shaped(CX + OV, CY + OV, NZ)
    local = pltpu.CompilerParams(vmem_limit_bytes=32 * 1024 * 1024)
    field, cover = pl.pallas_call(
        place_kernel,
        out_shape=[cells, cells],
        in_specs=[SM] * 3 + [pl.BlockSpec(memory_space=pltpu.VMEM)],
        out_specs=[pl.BlockSpec(memory_space=pltpu.VMEM)] * 2,
        compiler_params=local,
    )(corners, grain_ids, misfit, eta)
    scratch = [
        *[pltpu.VMEM(a.shape, a.dtype) for a in arrays],
        dma((len(arrays),)),
        dma((3,)),
        dma((boxes + 2,)),
        pltpu.VMEM((boxes, 32, 32, NZ), F32),
        pltpu.VMEM((boxes, 32, 32, NZ), F32),
        *[patch] * 4,
        pltpu.VMEM((CX, CY, NZ), F32),
        pltpu.VMEM((2, NX, 128), F32),
        pltpu.VMEM((2, NX, 128), F32),
        *[pltpu.VMEM((2, PY, KX, 128), F32)] * 4,
        pltpu.VMEM((2, NX, 128), F32),
        pltpu.VMEM((2, NX, 128), F32),
        *[pltpu.VMEM((NX, NX), BF16)] * 4,
        *[pltpu.VMEM((KX, NY), F32)] * 3,
        *[pltpu.VMEM((8, NY), F32)] * 3,
        pltpu.VMEM((2, KX, NY), F32),
        pltpu.VMEM((8, NY), F32),
        *[pltpu.VMEM((208, NY), BF16)] * 2,
        *[pltpu.VMEM((NX, 256), BF16)] * 2,
        pltpu.VMEM((CX, CY, NZ), F32),
        pltpu.VMEM((CX + OV, 8, NZ), F32),
        pltpu.VMEM((CX + OV, 16, NZ), F32),
        pltpu.VMEM((12, CY, NZ), F32),
        pltpu.VMEM((12, CY, NZ), F32),
        pltpu.VMEM((CX + OV, OV, NZ), F32),
        pltpu.VMEM((24, CY, NZ), F32),
        pltpu.VMEM((24, CY, NZ), F32),
        dma((2, 8)),
        dma((2, 8)),
        dma((6,)),
        dma((6,)),
        *[dma((2, 2))] * 4,
    ]
    hbm = pl.BlockSpec(memory_space=pl.ANY)
    base, mu, total = pl.pallas_call(
        mega_kernel,
        out_shape=[shaped(*eta.shape), cells, cells],
        in_specs=[hbm] * (3 + len(arrays)),
        out_specs=[hbm] * 3,
        scratch_shapes=scratch,
        compiler_params=pltpu.CompilerParams(
            vmem_limit_bytes=56 * 1024 * 1024, collective_id=0, has_side_effects=True
        ),
    )(eta, field, cover, *arrays)
    block = pl.BlockSpec((1, 32, 32, NZ), lambda b: (b, 0, 0, 0))
    window = pl.BlockSpec((CX + OV, CY + OV, NZ), lambda b: (0, 0, 0))
    return pl.pallas_call(
        final_kernel,
        grid=(boxes,),
        out_shape=[shaped(*eta.shape), shaped(CX, CY, NZ)],
        in_specs=[SM] * 3 + [block, block, window, window],
        out_specs=[block, pl.BlockSpec((CX, CY, NZ), lambda b: (0, 0, 0))],
        compiler_params=local,
    )(corners, grain_ids, misfit, eta, base, mu, total)


def solution(mesh):
    in_specs = (P(("px", "py"), None, None, None), P(("px", "py"), None), P(("px", "py")), P(), P("px", "py", None))
    out_specs = (P(("px", "py"), None, None, None), P("px", "py", None))
    return jax.shard_map(on_device, mesh=mesh, in_specs=in_specs, out_specs=out_specs, check_vma=False)
```

```python
import functools

import jax
import jax.numpy as jnp
import numpy as np
from jax import lax
from jax.experimental import pallas as pl
from jax.experimental.pallas import tpu as pltpu
from jax.sharding import PartitionSpec as P

NX, NY, NZ = 768, 512, 128
STEP = 8
PX, PY = 32, 8
CX, CY = NX // PX, NY // PY
OV = 24
KX = NX // PY
F32 = jnp.float32
BF16 = jnp.bfloat16
SPECIAL = 16
RATE = 0.2
GRADIENT = 0.1
COUPLING = 1.5

SM = pl.BlockSpec(memory_space=pltpu.SMEM)


def halves(array):
    high = np.asarray(array, np.float32).astype(jnp.bfloat16)
    low = (np.asarray(array, np.float64) - high.astype(np.float64)).astype(jnp.bfloat16)
    return high, low


def slot_wave(p, h):
    if h == 0:
        return 4 * p + 1
    return 4 * p + 2 if p < 16 else 4 * p


def depth_tables():
    z = np.arange(NZ)
    forward = np.zeros((NZ, NZ))
    inverse = np.zeros((NZ, NZ))
    total = NX * NY * NZ
    for h in range(2):
        for p in range(PX):
            row_re, row_im = h * 64 + p, h * 64 + 32 + p
            wave = slot_wave(p, h)
            cosine = np.cos(2 * np.pi * ((wave * z) % NZ) / NZ)
            sine = np.sin(2 * np.pi * ((wave * z) % NZ) / NZ)
            if p == SPECIAL and h == 1:
                forward[row_re], forward[row_im] = 1.0, (-1.0) ** z
                inverse[row_re], inverse[row_im] = 1.0 / total, (-1.0) ** z / total
            else:
                forward[row_re], forward[row_im] = cosine, -sine
                inverse[row_re], inverse[row_im] = 2 * cosine / total, -2 * sine / total
    return forward, inverse


def wave_rows(count, step, length):
    angle = 2 * np.pi * ((step * np.arange(count)[:, None] * np.arange(length)[None]) % length) / length
    return np.stack([np.cos(angle), np.sin(angle)]).astype(np.float32)


def seed_tables():
    seeds = np.zeros((2, 104, NX), np.float32)
    seeds[:, 0:24] = wave_rows(24, 32, NX)
    seeds[:, 24:56] = wave_rows(32, 1, NX)
    seeds[:, 56:72, :NY] = wave_rows(16, 32, NY)
    seeds[:, 72:104, :NY] = wave_rows(32, 1, NY)
    return seeds


def split(value):
    high = value.astype(BF16)
    return high, (value - high.astype(F32)).astype(BF16)


def dot(a, b):
    return jnp.dot(a, b, preferred_element_type=F32)


def dot3(a, b):
    return dot(a[0], b[0]) + dot(a[0], b[1]) + dot(a[1], b[0])


def turn(value):
    return pltpu.roll(value, 64, axis=value.ndim - 1)


def low_lanes(shape):
    return lax.broadcasted_iota(jnp.int32, shape, len(shape) - 1) < 64


def shaped(*shape, dtype=F32):
    return jax.ShapeDtypeStruct(shape, dtype)


MESH = pl.DeviceIdType.MESH
CUT_X = ((0, 12), (12, 36), (36, 48))
CUT_Y = ((0, 8), (8, 72), (72, 88))
TAKE_X = ((0, 12), (0, 24), (12, 24))
TAKE_Y = ((0, 16), (0, 64), (56, 64))
GIVE_X = ((36, 48), (12, 36), (0, 12))
GIVE_Y = ((72, 88), (8, 72), (0, 8))
AROUND = [(a, b) for a, b in ((0, 1), (2, 1), (1, 0), (1, 2), (0, 0), (0, 2), (2, 0), (2, 2))]


def box(ref, x, y):
    return ref.at[pl.ds(x[0], x[1] - x[0]), pl.ds(y[0], y[1] - y[0])]


def wrap(value, count):
    return (value + count) % count


def push(source, target, send, receive, p, q):
    return pltpu.make_async_remote_copy(
        src_ref=source, dst_ref=target, send_sem=send, recv_sem=receive, device_id=(p, q), device_id_type=MESH
    )


def drain(ref, semaphore):
    pltpu.make_async_copy(ref, ref, semaphore).wait()


def mega_kernel(
    eta, field, cover, green, seeds, waves_in,
    result, mu_window, oc_window,
    table_h, table_l, cut_low, cut_high, summed,
    grid, s1, r1, y1, t1, y2, t2, s2, r2, cos_h, cos_l, sin_h, sin_l,
    near, far, extra, near_row, far_row, extra_row, gs, gx, work_h, work_l, one_h, two_h, potential,
    low_y, high_y, low_x, high_x, side_o, low_o, high_o, halo_send, halo_recv, green_send, green_recv, px_send, px_recv, py_send, py_recv,
):
    p, q = lax.axis_index("px"), lax.axis_index("py")
    upper_half = p // 16
    far_to = 31 - p + (1 - upper_half) - 16 * (1 - (p + 31) // 32)
    far_from = 31 - p + upper_half - 16 * upper_half * (1 - (p + 15) // 32)
    flip, flip_row = 7 - q, (8 - q) % 8

    boxes = eta.shape[0]
    barrier = pltpu.get_barrier_semaphore()

    def greet(a, b):
        pl.semaphore_signal(barrier, inc=1, device_id=(a, b), device_id_type=MESH)

    @pl.loop(1, PX)
    def _(j):
        greet((p + j) % PX, q)

    @pl.loop(1, PY)
    def _(j):
        greet(p, (q + j) % PY)

    for a in (-1, 1):
        for b in (-1, 1):
            greet(wrap(p + a, PX), wrap(q + b, PY))
    greet(31 - p, flip)
    greet(31 - p, flip_row)
    greet(far_from, flip)
    greet(far_from, flip_row)
    pl.semaphore_wait(barrier, (PX - 1) + (PY - 1) + 8)

    def spread(source, window, group):
        copies = []
        for n, (a, b) in enumerate(AROUND):
            copy = push(
                box(source, TAKE_X[a], TAKE_Y[b]), box(window, GIVE_X[a], GIVE_Y[b]),
                halo_send.at[group, n], halo_recv.at[group, n], wrap(p + a - 1, PX), wrap(q + b - 1, PY),
            )
            copy.start()
            copies.append(copy)
        box(window, CUT_X[1], CUT_Y[1])[...] = source[...]
        return copies

    near_copies = [
        push(green.at[3], near, green_send.at[0], green_recv.at[0], 31 - p, flip),
        push(green.at[3, pl.ds(0, 8)], near_row, green_send.at[2], green_recv.at[2], 31 - p, flip_row),
    ]
    far_copies = [
        push(green.at[2 * upper_half], far, green_send.at[1], green_recv.at[1], far_to, flip),
        push(green.at[2 * upper_half, pl.ds(0, 8)], far_row, green_send.at[3], green_recv.at[3], far_to, flip_row),
    ]
    for copy in near_copies:
        copy.start()
    pending = near_copies + far_copies
    next_p, last_p, next_q, last_q = wrap(p + 1, PX), wrap(p - 1, PX), wrap(q + 1, PY), wrap(q - 1, PY)

    def halo(source, target, slot, a, b):
        copy = push(source, target, halo_send.at[0, slot], halo_recv.at[0, slot], a, b)
        pending.append(copy)
        return copy

    along_y = [
        halo(field.at[:, pl.ds(0, 8)], low_y, 0, p, last_q),
        halo(field.at[:, pl.ds(72, 16)], high_y, 1, p, next_q),
    ]
    for copy in along_y:
        copy.start()
    side_copy = halo(cover.at[:, pl.ds(CY, OV)], side_o, 2, p, next_q)
    side_copy.start()
    for copy in along_y:
        copy.wait_recv()

    def joined(target, rows):
        target[...] = field[rows, 8 : 8 + CY]
        target[:, 0:16] = target[:, 0:16] + high_y[rows]
        target[:, 56:64] = target[:, 56:64] + low_y[rows]

    joined(cut_low, slice(0, 12))
    joined(cut_high, slice(36, 48))
    along_x = [halo(cut_low, low_x, 3, last_p, q), halo(cut_high, high_x, 4, next_p, q)]
    for copy in along_x:
        copy.start()
    joined(grid, slice(12, 36))

    def extra_copy(a, b):
        return push(green.at[0], extra, green_send.at[4], green_recv.at[4], a, b)

    def extra_row_copy():
        return push(green.at[0, pl.ds(0, 8)], extra_row, green_send.at[5], green_recv.at[5], SPECIAL, flip_row)

    sends_extra = ((p == 0) | (p == SPECIAL)) & (q < 4)
    sends_row = (p == SPECIAL) & (q > 0) & (q < 4)
    extra_to = q + (p // SPECIAL) * (flip - q)

    fine_c, fine_s = seeds[0, 24:56], seeds[1, 24:56]

    def table_body(k, unused):
        coarse_c, coarse_s = seeds[0, pl.ds(k, 1), :], seeds[1, pl.ds(k, 1), :]
        rows = pl.ds(pl.multiple_of(32 * k, 32), 32)
        cos_h[rows, :], cos_l[rows, :] = split(coarse_c * fine_c - coarse_s * fine_s)
        sin_h[rows, :], sin_l[rows, :] = split(coarse_s * fine_c + coarse_c * fine_s)
        return unused

    lax.fori_loop(0, NX // 32, table_body, 0)
    short_c, short_s = seeds[0, 72:104, :NY], seeds[1, 72:104, :NY]

    def column_body(k, unused):
        coarse_c, coarse_s = seeds[0, pl.ds(56 + k, 1), :NY], seeds[1, pl.ds(56 + k, 1), :NY]
        rows = pl.ds(pl.multiple_of(32 * k, 32), 32)
        table_h[rows, 0:NY], table_l[rows, 0:NY] = split(coarse_c * short_c - coarse_s * short_s)
        table_h[rows, NY:], table_l[rows, NY:] = split(coarse_s * short_c + coarse_c * short_s)
        return unused

    lax.fori_loop(0, NY // 32, column_body, 0)

    for copy in along_x:
        copy.wait_recv()
    grid[0:12] = grid[0:12] + high_x[...]
    grid[12:24] = grid[12:24] + low_x[...]

    keep = low_lanes((PX, 128))
    nt = (((1,), (1,)), ((), ()))
    for h in range(2):
        waves = (waves_in[64 * h : 64 * h + 64], waves_in[128 + 64 * h : 192 + 64 * h])
        for group in range(CX // 4):
            rows = split(grid[4 * group : 4 * group + 4].reshape(256, NZ))
            spectrum = (
                lax.dot_general(waves[0], rows[0], nt, preferred_element_type=F32)
                + lax.dot_general(waves[0], rows[1], nt, preferred_element_type=F32)
                + lax.dot_general(waves[1], rows[0], nt, preferred_element_type=F32)
            )
            for tile in range(2):
                real = spectrum[0:32, 128 * tile : 128 * tile + 128]
                imag = spectrum[32:64, 128 * tile : 128 * tile + 128]
                x = 4 * group + 2 * tile
                s1.at[h][pl.ds(x, PX, stride=24), :] = jnp.where(keep, real, turn(imag))
                s1.at[h][pl.ds(x + 1, PX, stride=24), :] = jnp.where(keep, turn(real), imag)

        @pl.loop(1, PX)
        def _(j):
            to = (p + j) % PX
            rows = pl.ds(pl.multiple_of(24 * to, 8), 24)
            here = pl.ds(pl.multiple_of(24 * p, 8), 24)
            push(s1.at[h, rows], r1.at[h, here], px_send.at[0, h], px_recv.at[0, h], to, q).start()

        here = pl.ds(pl.multiple_of(24 * p, 8), 24)
        r1[h, here, :] = s1[h, here, :]

    for copy in far_copies:
        copy.start()

    @pl.when(sends_extra)
    def _():
        extra_copy(SPECIAL, extra_to).start()

    @pl.when(sends_row)
    def _():
        extra_row_copy().start()

    side_copy.wait_recv()
    summed[...] = cover[:, 0:CY]
    summed[:, 0:OV] = summed[:, 0:OV] + side_o[...]
    cover_x = [
        halo(summed.at[pl.ds(0, 24)], low_o, 5, last_p, q),
        halo(summed.at[pl.ds(24, 24)], high_o, 6, next_p, q),
    ]
    for copy in cover_x:
        copy.start()

    def opposite(count):
        places = lax.broadcasted_iota(jnp.int32, (count, count), 0) + lax.broadcasted_iota(jnp.int32, (count, count), 1)
        return places, jnp.where(places == count, 1.0, 0.0)

    flips = opposite(KX)[1].astype(BF16)
    places, lanes_flip = opposite(NY)
    lanes_flip = jnp.where(places == 0, 1.0, lanes_flip).astype(BF16)

    def permute(value):
        high, low = split(value)
        return dot(high, lanes_flip) + dot(low, lanes_flip)

    def mirror(plane, row):
        high, low = split(plane)
        turned = dot(flips, high) + dot(flips, low)
        first_row = lax.broadcasted_iota(jnp.int32, turned.shape, 0) == 0
        return permute(jnp.where(first_row, jnp.broadcast_to(row, turned.shape), turned))

    for copy in near_copies:
        copy.wait_recv()
    gs[0] = 0.5 * (green[1] + mirror(near[...], near_row[0:1]))

    keep = low_lanes((KX, 128))
    special = p == SPECIAL
    most = 31 * 24
    for h in range(2):
        drain(r1.at[h, pl.ds(0, most)], px_recv.at[0, h])
        high, low = split(r1[h])
        both_parts = jnp.concatenate([high, low], axis=1)
        one_h[...] = both_parts

        def rows_body(k, unused):
            rows = pl.ds(pl.multiple_of(KX * k, KX), KX)
            data = one_h[...]
            cosine = dot(cos_h[rows, :], data)
            cosine = cosine[:, :128] + cosine[:, 128:] + dot(cos_l[rows, :], data[:, :128])
            sine = dot(sin_h[rows, :], data)
            sine = sine[:, :128] + sine[:, 128:] + dot(sin_l[rows, :], data[:, :128])
            turned = turn(sine)
            value = jnp.where(keep, cosine + turned, cosine - turned)
            if h == 1:
                below = jnp.where(keep, cosine, -turned)
                above = jnp.where(keep, turn(cosine), -sine)
                parted = jnp.where(k < 4, below, above)
                top = (lax.broadcasted_iota(jnp.int32, (KX, 128), 0) == 0) & (k % 4 == 0)
                value = jnp.where(special & jnp.logical_not(top), parted, jnp.where(special, cosine, value))
            y1[h, k] = value

            @pl.when(k != q)
            def _():
                push(y1.at[h, k], t1.at[h, q], py_send.at[0, h], py_recv.at[0, h], p, k).start()

            return unused

        lax.fori_loop(0, PY, rows_body, 0)
        t1[h, q] = y1[h, q]

    packed = special & (q % 4 == 0)
    top = (lax.broadcasted_iota(jnp.int32, (KX, NY), 0) == 0) & packed

    def second_green():
        for copy in far_copies:
            copy.wait_recv()

        @pl.when(p == SPECIAL)
        def _():
            extra_copy(SPECIAL, extra_to).wait_recv()

        @pl.when((p == SPECIAL) & (q > 4))
        def _():
            extra_row_copy().wait_recv()

        upper = special & (q >= 4)
        lower = special & (q < 4)
        base = jnp.where(p < 16, green[2], jnp.where(lower, extra[...], green[0]))
        plane = jnp.where(upper, extra[...], far[...])
        row = jnp.where(upper, extra_row[0:1], far_row[0:1])
        half = 0.5 * (base + mirror(plane, row))
        packed_rows = jnp.concatenate(
            [jnp.broadcast_to(far_row[0:1], (8, NY)), jnp.broadcast_to(green[0, 0:1], (8, NY))], axis=0
        )
        packed_rows = 0.5 * (packed_rows + permute(packed_rows))
        gs[1] = jnp.where(top, jnp.broadcast_to(packed_rows[0:1], (KX, NY)), half)
        gx[...] = packed_rows[8:16]

    tables = (table_h[...], table_l[...])
    for h in range(2):
        if h == 1:
            second_green()
        drain(t1.at[h, pl.ds(0, PY - 1)], py_recv.at[0, h])
        for tile in range(4):
            even, odd = t1[h, 2 * tile], t1[h, 2 * tile + 1]
            lanes = slice(128 * tile, 128 * tile + 128)
            work_h[0:96, lanes], work_l[0:96, lanes] = split(jnp.where(keep, even, turn(odd)))
            work_h[96:192, lanes], work_l[96:192, lanes] = split(jnp.where(keep, turn(even), odd))
        wave = dot3((work_h[0:192], work_l[0:192]), tables)
        re_c, re_s = wave[0:96, :NY], wave[0:96, NY:]
        im_c, im_s = wave[96:192, :NY], wave[96:192, NY:]
        real, imag = re_c + im_s, im_c - re_s
        if h == 1:
            real, imag = jnp.where(top, re_c, real), jnp.where(top, -re_s, imag)
            fix = gx[...]
            work_h[192:200], work_l[192:200] = split(fix * im_c[0:8])
            work_h[200:208], work_l[200:208] = split(fix * -im_s[0:8])
        work_h[0:96], work_l[0:96] = split(gs[h] * real)
        work_h[96:192], work_l[96:192] = split(gs[h] * imag)
        used = slice(0, 208 if h == 1 else 192)
        wave = dot3((work_h[used], work_l[used]), tables)
        real = wave[0:96, :NY] - wave[96:192, NY:]
        imag = wave[96:192, :NY] + wave[0:96, NY:]
        if h == 1:
            fix = wave[192:200, :NY] - wave[200:208, NY:]
            imag = jnp.where(top, jnp.broadcast_to(fix[0:1], (KX, NY)), imag)
        for tile in range(4):
            lanes = slice(128 * tile, 128 * tile + 128)
            re, im = real[:, lanes], imag[:, lanes]
            y2[h, 2 * tile] = jnp.where(keep, re, turn(im))
            y2[h, 2 * tile + 1] = jnp.where(keep, turn(re), im)

        @pl.loop(1, PY)
        def _(j):
            to = (q + j) % PY
            push(y2.at[h, to], t2.at[h, q], py_send.at[1, h], py_recv.at[1, h], p, to).start()

        t2[h, q] = y2[h, q]

    for copy in cover_x:
        copy.wait_recv()
    oc_window[0:24, 0:CY] = summed[0:24] + high_o[...]
    oc_window[24:48, 0:CY] = summed[24:48] + low_o[...]
    cover_y = halo(oc_window.at[:, pl.ds(0, OV)], oc_window.at[:, pl.ds(CY, OV)], 7, p, last_q)
    cover_y.start()

    for h in range(2):
        drain(t2.at[h, pl.ds(0, PY - 1)], py_recv.at[1, h])
        for k in range(PY):
            value = t2[h, k]
            turned = turn(value)
            one = value
            two = jnp.where(keep, -turned, turned)
            if h == 1:
                if k < 4:
                    one_s, two_s = jnp.where(keep, 2.0 * value, 0.0), jnp.where(keep, -2.0 * turned, 0.0)
                else:
                    one_s, two_s = jnp.where(keep, 0.0, 2.0 * turned), jnp.where(keep, 0.0, -2.0 * value)
                if k % 4 == 0:
                    row_zero = lax.broadcasted_iota(jnp.int32, (KX, 128), 0) == 0
                    one_s, two_s = jnp.where(row_zero, value, one_s), jnp.where(row_zero, 0.0, two_s)
                one, two = jnp.where(special, one_s, one), jnp.where(special, two_s, two)
            rows = slice(KX * k, KX * k + KX)
            one_h[rows, 0:128], one_h[rows, 128:256] = split(one)
            two_h[rows, 0:128], two_h[rows, 128:256] = split(two)

        def unrows_body(k, unused):
            rows = pl.ds(pl.multiple_of(KX * k, KX), KX)
            one, two = one_h[...], two_h[...]
            result = dot(cos_h[rows, :], one) + dot(sin_h[rows, :], two)
            result = result[:, :128] + result[:, 128:] + dot(cos_l[rows, :], one[:, :128]) + dot(sin_l[rows, :], two[:, :128])
            s2[h, rows, :] = result
            for i in range(4):
                to = 4 * k + i

                @pl.when(to != p)
                def _():
                    part = pl.ds(pl.multiple_of(24 * to, 8), 24)
                    here = pl.ds(pl.multiple_of(24 * p, 8), 24)
                    push(s2.at[h, part], r2.at[h, here], px_send.at[1, h], px_recv.at[1, h], to, q).start()

            return unused

        lax.fori_loop(0, 8, unrows_body, 0)
        here = pl.ds(pl.multiple_of(24 * p, 8), 24)
        r2[h, here, :] = s2[h, here, :]

    cover_y.wait_recv()
    sublane = lax.broadcasted_iota(jnp.int32, (32, NZ), 0)
    for b in range(boxes):

        def base_body(i, unused):
            value = eta[b, i]
            before = jnp.where(i > 0, eta[b, jnp.maximum(i - 1, 0)], 0.0)
            after = jnp.where(i < 31, eta[b, jnp.minimum(i + 1, 31)], 0.0)
            above = jnp.where(sublane == 0, 0.0, pltpu.roll(value, 1, axis=0))
            below = jnp.where(sublane == 31, 0.0, pltpu.roll(value, 31, axis=0))
            lap = before + after + above + below + pltpu.roll(value, 1, axis=1) + pltpu.roll(value, 127, axis=1)
            lap = lap - 6.0 * value
            square = value * value
            force = value * square - value - 2.0 * COUPLING * value * square - GRADIENT * lap
            result[b, i] = value - RATE * force
            return unused

        lax.fori_loop(0, 32, base_body, 0, unroll=2)

    keep = low_lanes((PX, 128))
    for h in range(2):
        drain(r2.at[h, pl.ds(0, most)], px_recv.at[1, h])
        waves = (waves_in[256 + 64 * h : 320 + 64 * h], waves_in[384 + 64 * h : 448 + 64 * h])
        for tile in range(CX // 2):
            x = 2 * tile
            even = r2.at[h][pl.ds(x, PX, stride=24), :]
            odd = r2.at[h][pl.ds(x + 1, PX, stride=24), :]
            parts = [jnp.where(keep, even, turn(odd)), jnp.where(keep, turn(even), odd)]
            block = split(jnp.concatenate(parts, axis=0).T)
            value = dot3(block, waves).reshape(2, CY, NZ)
            if h == 0:
                potential[x : x + 2] = value
            else:
                potential[x : x + 2] = potential[x : x + 2] + value

    around = spread(potential, mu_window, 1)
    pending += around
    for copy in around:
        copy.wait_recv()
    for copy in pending:
        copy.wait_send()

    @pl.when(sends_extra)
    def _():
        extra_copy(SPECIAL, extra_to).wait_send()

    @pl.when(sends_row)
    def _():
        extra_row_copy().wait_send()

    for h in range(2):
        drain(s1.at[h, pl.ds(0, most)], px_send.at[0, h])
        drain(s2.at[h, pl.ds(0, most)], px_send.at[1, h])
        drain(y1.at[h, pl.ds(0, PY - 1)], py_send.at[0, h])
        drain(y2.at[h, pl.ds(0, PY - 1)], py_send.at[1, h])


def place_kernel(corners, ids, misfit, eta, field, cover):
    shift_x, shift_y = lax.axis_index("px") * CX, lax.axis_index("py") * CY
    field[...] = jnp.zeros_like(field)
    cover[...] = jnp.zeros_like(cover)
    for b in range(eta.shape[0]):
        weight = misfit[ids[b]]
        sx = corners[b, 0] * STEP - shift_x
        sy = pl.multiple_of(corners[b, 1] * STEP - shift_y, 8)

        def body(i, unused):
            value = eta[b, i]
            square = value * value
            rows = pl.ds(sy, 32)
            field[sx + i, rows, :] = field[sx + i, rows, :] + weight * square
            cover[sx + i, rows, :] = cover[sx + i, rows, :] + square
            return unused

        lax.fori_loop(0, 32, body, 0, unroll=4)


def final_kernel(corners, ids, misfit, eta, base, mu_window, oc_window, out, potential):
    b = pl.program_id(0)
    shift_x, shift_y = lax.axis_index("px") * CX, lax.axis_index("py") * CY

    @pl.when(b == 0)
    def _():
        potential[...] = mu_window[:CX, :CY]

    factor = 2.0 * RATE * misfit[ids[b]]
    sx = corners[b, 0] * STEP - shift_x
    sy = pl.multiple_of(corners[b, 1] * STEP - shift_y, 8)

    def body(i, unused):
        rows = pl.ds(sy, 32)
        mu = mu_window[sx + i, rows, :]
        total = oc_window[sx + i, rows, :]
        out[0, i] = base[0, i] - eta[0, i] * (2.0 * RATE * COUPLING * total + factor * mu)
        return unused

    lax.fori_loop(0, 32, body, 0, unroll=4)


def on_device(eta, corners, grain_ids, misfit, green):
    forward, inverse = depth_tables()
    dma = pltpu.SemaphoreType.DMA
    arrays = [green, seed_tables(), np.concatenate([*halves(forward), *halves(inverse)])]
    boxes = eta.shape[0]
    vmem = pl.BlockSpec(memory_space=pltpu.VMEM)
    cells = shaped(CX + OV, CY + OV, NZ)
    local = pltpu.CompilerParams(vmem_limit_bytes=24 * 1024 * 1024)
    field, cover = pl.pallas_call(
        place_kernel,
        out_shape=[cells, cells],
        in_specs=[SM] * 3 + [pl.BlockSpec(memory_space=pltpu.VMEM)],
        out_specs=[pl.BlockSpec(memory_space=pltpu.VMEM)] * 2,
        compiler_params=local,
    )(corners, grain_ids, misfit, eta)
    scratch = [
        pltpu.VMEM((NY, 2 * NY), BF16),
        pltpu.VMEM((NY, 2 * NY), BF16),
        pltpu.VMEM((12, CY, NZ), F32),
        pltpu.VMEM((12, CY, NZ), F32),
        pltpu.VMEM((CX + OV, CY, NZ), F32),
        pltpu.VMEM((CX, CY, NZ), F32),
        pltpu.VMEM((2, NX, 128), F32),
        pltpu.VMEM((2, NX, 128), F32),
        *[pltpu.VMEM((2, PY, KX, 128), F32)] * 4,
        pltpu.VMEM((2, NX, 128), F32),
        pltpu.VMEM((2, NX, 128), F32),
        *[pltpu.VMEM((NX, NX), BF16)] * 4,
        *[pltpu.VMEM((KX, NY), F32)] * 3,
        *[pltpu.VMEM((8, NY), F32)] * 3,
        pltpu.VMEM((2, KX, NY), F32),
        pltpu.VMEM((8, NY), F32),
        *[pltpu.VMEM((208, NY), BF16)] * 2,
        *[pltpu.VMEM((NX, 256), BF16)] * 2,
        pltpu.VMEM((CX, CY, NZ), F32),
        pltpu.VMEM((CX + OV, 8, NZ), F32),
        pltpu.VMEM((CX + OV, 16, NZ), F32),
        pltpu.VMEM((12, CY, NZ), F32),
        pltpu.VMEM((12, CY, NZ), F32),
        pltpu.VMEM((CX + OV, OV, NZ), F32),
        pltpu.VMEM((24, CY, NZ), F32),
        pltpu.VMEM((24, CY, NZ), F32),
        dma((2, 8)),
        dma((2, 8)),
        dma((6,)),
        dma((6,)),
        *[dma((2, 2))] * 4,
    ]
    base, mu, total = pl.pallas_call(
        mega_kernel,
        out_shape=[shaped(*eta.shape), cells, cells],
        in_specs=[vmem] * (3 + len(arrays)),
        out_specs=[vmem] * 3,
        scratch_shapes=scratch,
        compiler_params=pltpu.CompilerParams(
            vmem_limit_bytes=36 * 1024 * 1024, collective_id=0, has_side_effects=True
        ),
    )(eta, field, cover, *arrays)
    block = pl.BlockSpec((1, 32, 32, NZ), lambda b: (b, 0, 0, 0))
    window = pl.BlockSpec((CX + OV, CY + OV, NZ), lambda b: (0, 0, 0))
    return pl.pallas_call(
        final_kernel,
        grid=(boxes,),
        out_shape=[shaped(*eta.shape), shaped(CX, CY, NZ)],
        in_specs=[SM] * 3 + [block, block, window, window],
        out_specs=[block, pl.BlockSpec((CX, CY, NZ), lambda b: (0, 0, 0))],
        compiler_params=local,
    )(corners, grain_ids, misfit, eta, base, mu, total)


def solution(mesh):
    in_specs = (P(("px", "py"), None, None, None), P(("px", "py"), None), P(("px", "py")), P(), P("px", "py", None))
    out_specs = (P(("px", "py"), None, None, None), P("px", "py", None))
    return jax.shard_map(on_device, mesh=mesh, in_specs=in_specs, out_specs=out_specs, check_vma=False)
```

```python
import functools

import jax
import jax.numpy as jnp
import numpy as np
from jax import lax
from jax.experimental import pallas as pl
from jax.experimental.pallas import tpu as pltpu
from jax.sharding import PartitionSpec as P

NX, NY, NZ = 768, 512, 128
STEP = 8
PX, PY = 32, 8
CX, CY = NX // PX, NY // PY
OV = 24
KX = NX // PY
F32 = jnp.float32
BF16 = jnp.bfloat16
SPECIAL = 16
RATE = 0.2
GRADIENT = 0.1
COUPLING = 1.5

SM = pl.BlockSpec(memory_space=pltpu.SMEM)


def halves(array):
    high = np.asarray(array, np.float32).astype(jnp.bfloat16)
    low = (np.asarray(array, np.float64) - high.astype(np.float64)).astype(jnp.bfloat16)
    return high, low


def slot_wave(p, h):
    if h == 0:
        return 4 * p + 1
    return 4 * p + 2 if p < 16 else 4 * p


def depth_tables():
    z = np.arange(NZ)
    forward = np.zeros((NZ, NZ))
    inverse = np.zeros((NZ, NZ))
    total = NX * NY * NZ
    for h in range(2):
        for p in range(PX):
            row_re, row_im = h * 64 + p, h * 64 + 32 + p
            wave = slot_wave(p, h)
            cosine = np.cos(2 * np.pi * ((wave * z) % NZ) / NZ)
            sine = np.sin(2 * np.pi * ((wave * z) % NZ) / NZ)
            if p == SPECIAL and h == 1:
                forward[row_re], forward[row_im] = 1.0, (-1.0) ** z
                inverse[row_re], inverse[row_im] = 1.0 / total, (-1.0) ** z / total
            else:
                forward[row_re], forward[row_im] = cosine, -sine
                inverse[row_re], inverse[row_im] = 2 * cosine / total, -2 * sine / total
    return forward, inverse


def wave_rows(count, step, length):
    angle = 2 * np.pi * ((step * np.arange(count)[:, None] * np.arange(length)[None]) % length) / length
    return np.stack([np.cos(angle), np.sin(angle)]).astype(np.float32)


def seed_tables():
    seeds = np.zeros((2, 104, NX), np.float32)
    seeds[:, 0:24] = wave_rows(24, 32, NX)
    seeds[:, 24:56] = wave_rows(32, 1, NX)
    seeds[:, 56:72, :NY] = wave_rows(16, 32, NY)
    seeds[:, 72:104, :NY] = wave_rows(32, 1, NY)
    return seeds


def split(value):
    high = value.astype(BF16)
    return high, (value - high.astype(F32)).astype(BF16)


def dot(a, b):
    return jnp.dot(a, b, preferred_element_type=F32)


def dot3(a, b):
    return dot(a[0], b[0]) + dot(a[0], b[1]) + dot(a[1], b[0])


def turn(value):
    return pltpu.roll(value, 64, axis=value.ndim - 1)


def low_lanes(shape):
    return lax.broadcasted_iota(jnp.int32, shape, len(shape) - 1) < 64


def shaped(*shape, dtype=F32):
    return jax.ShapeDtypeStruct(shape, dtype)


MESH = pl.DeviceIdType.MESH
CUT_X = ((0, 12), (12, 36), (36, 48))
CUT_Y = ((0, 8), (8, 72), (72, 88))
TAKE_X = ((0, 12), (0, 24), (12, 24))
TAKE_Y = ((0, 16), (0, 64), (56, 64))
GIVE_X = ((36, 48), (12, 36), (0, 12))
GIVE_Y = ((72, 88), (8, 72), (0, 8))
AROUND = [(a, b) for a, b in ((0, 1), (2, 1), (1, 0), (1, 2), (0, 0), (0, 2), (2, 0), (2, 2))]


def box(ref, x, y):
    return ref.at[pl.ds(x[0], x[1] - x[0]), pl.ds(y[0], y[1] - y[0])]


def wrap(value, count):
    return (value + count) % count


def push(source, target, send, receive, p, q):
    return pltpu.make_async_remote_copy(
        src_ref=source, dst_ref=target, send_sem=send, recv_sem=receive, device_id=(p, q), device_id_type=MESH
    )


def drain(ref, semaphore):
    pltpu.make_async_copy(ref, ref, semaphore).wait()


def mega_kernel(
    eta, field, cover, green, seeds, waves_in,
    result, mu_window, oc_window,
    table_h, table_l, cut_low, cut_high, summed,
    grid, s1, r1, y1, t1, y2, t2, s2, r2, cos_h, cos_l, sin_h, sin_l,
    near, far, extra, near_row, far_row, extra_row, gs, gx, work_h, work_l, one_h, two_h, potential,
    low_y, high_y, low_x, high_x, side_o, low_o, high_o, halo_send, halo_recv, green_send, green_recv, px_send, px_recv, py_send, py_recv,
):
    p, q = lax.axis_index("px"), lax.axis_index("py")
    upper_half = p // 16
    far_to = 31 - p + (1 - upper_half) - 16 * (1 - (p + 31) // 32)
    far_from = 31 - p + upper_half - 16 * upper_half * (1 - (p + 15) // 32)
    flip, flip_row = 7 - q, (8 - q) % 8

    boxes = eta.shape[0]
    barrier = pltpu.get_barrier_semaphore()

    def greet(a, b):
        pl.semaphore_signal(barrier, inc=1, device_id=(a, b), device_id_type=MESH)

    @pl.loop(1, PX)
    def _(j):
        greet((p + j) % PX, q)

    @pl.loop(1, PY)
    def _(j):
        greet(p, (q + j) % PY)

    for a in (-1, 1):
        for b in (-1, 1):
            greet(wrap(p + a, PX), wrap(q + b, PY))
    greet(31 - p, flip)
    greet(31 - p, flip_row)
    greet(far_from, flip)
    greet(far_from, flip_row)
    pl.semaphore_wait(barrier, (PX - 1) + (PY - 1) + 8)

    def spread(source, window, group):
        copies = []
        for n, (a, b) in enumerate(AROUND):
            copy = push(
                box(source, TAKE_X[a], TAKE_Y[b]), box(window, GIVE_X[a], GIVE_Y[b]),
                halo_send.at[group, n], halo_recv.at[group, n], wrap(p + a - 1, PX), wrap(q + b - 1, PY),
            )
            copy.start()
            copies.append(copy)
        box(window, CUT_X[1], CUT_Y[1])[...] = source[...]
        return copies

    near_copies = [
        push(green.at[3], near, green_send.at[0], green_recv.at[0], 31 - p, flip),
        push(green.at[3, pl.ds(0, 8)], near_row, green_send.at[2], green_recv.at[2], 31 - p, flip_row),
    ]
    far_copies = [
        push(green.at[2 * upper_half], far, green_send.at[1], green_recv.at[1], far_to, flip),
        push(green.at[2 * upper_half, pl.ds(0, 8)], far_row, green_send.at[3], green_recv.at[3], far_to, flip_row),
    ]
    for copy in near_copies:
        copy.start()
    pending = near_copies + far_copies
    next_p, last_p, next_q, last_q = wrap(p + 1, PX), wrap(p - 1, PX), wrap(q + 1, PY), wrap(q - 1, PY)

    def halo(source, target, slot, a, b):
        copy = push(source, target, halo_send.at[0, slot], halo_recv.at[0, slot], a, b)
        pending.append(copy)
        return copy

    along_y = [
        halo(field.at[:, pl.ds(0, 8)], low_y, 0, p, last_q),
        halo(field.at[:, pl.ds(72, 16)], high_y, 1, p, next_q),
    ]
    for copy in along_y:
        copy.start()
    side_copy = halo(cover.at[:, pl.ds(CY, OV)], side_o, 2, p, next_q)
    side_copy.start()
    for copy in along_y:
        copy.wait_recv()

    def joined(target, rows):
        target[...] = field[rows, 8 : 8 + CY]
        target[:, 0:16] = target[:, 0:16] + high_y[rows]
        target[:, 56:64] = target[:, 56:64] + low_y[rows]

    joined(cut_low, slice(0, 12))
    joined(cut_high, slice(36, 48))
    along_x = [halo(cut_low, low_x, 3, last_p, q), halo(cut_high, high_x, 4, next_p, q)]
    for copy in along_x:
        copy.start()
    joined(grid, slice(12, 36))

    def extra_copy(a, b):
        return push(green.at[0], extra, green_send.at[4], green_recv.at[4], a, b)

    def extra_row_copy():
        return push(green.at[0, pl.ds(0, 8)], extra_row, green_send.at[5], green_recv.at[5], SPECIAL, flip_row)

    sends_extra = ((p == 0) | (p == SPECIAL)) & (q < 4)
    sends_row = (p == SPECIAL) & (q > 0) & (q < 4)
    extra_to = q + (p // SPECIAL) * (flip - q)

    fine_c, fine_s = seeds[0, 24:56], seeds[1, 24:56]

    def table_body(k, unused):
        coarse_c, coarse_s = seeds[0, pl.ds(k, 1), :], seeds[1, pl.ds(k, 1), :]
        rows = pl.ds(pl.multiple_of(32 * k, 32), 32)
        cos_h[rows, :], cos_l[rows, :] = split(coarse_c * fine_c - coarse_s * fine_s)
        sin_h[rows, :], sin_l[rows, :] = split(coarse_s * fine_c + coarse_c * fine_s)
        return unused

    lax.fori_loop(0, NX // 32, table_body, 0)
    short_c, short_s = seeds[0, 72:104, :NY], seeds[1, 72:104, :NY]

    def column_body(k, unused):
        coarse_c, coarse_s = seeds[0, pl.ds(56 + k, 1), :NY], seeds[1, pl.ds(56 + k, 1), :NY]
        rows = pl.ds(pl.multiple_of(32 * k, 32), 32)
        table_h[rows, 0:NY], table_l[rows, 0:NY] = split(coarse_c * short_c - coarse_s * short_s)
        table_h[rows, NY:], table_l[rows, NY:] = split(coarse_s * short_c + coarse_c * short_s)
        return unused

    lax.fori_loop(0, NY // 32, column_body, 0)

    for copy in along_x:
        copy.wait_recv()
    grid[0:12] = grid[0:12] + high_x[...]
    grid[12:24] = grid[12:24] + low_x[...]

    keep = low_lanes((PX, 128))
    nt = (((1,), (1,)), ((), ()))
    for h in range(2):
        waves = (waves_in[64 * h : 64 * h + 64], waves_in[128 + 64 * h : 192 + 64 * h])
        for group in range(CX // 4):
            rows = split(grid[4 * group : 4 * group + 4].reshape(256, NZ))
            spectrum = (
                lax.dot_general(waves[0], rows[0], nt, preferred_element_type=F32)
                + lax.dot_general(waves[0], rows[1], nt, preferred_element_type=F32)
                + lax.dot_general(waves[1], rows[0], nt, preferred_element_type=F32)
            )
            for tile in range(2):
                real = spectrum[0:32, 128 * tile : 128 * tile + 128]
                imag = spectrum[32:64, 128 * tile : 128 * tile + 128]
                x = 4 * group + 2 * tile
                s1.at[h][pl.ds(x, PX, stride=24), :] = jnp.where(keep, real, turn(imag))
                s1.at[h][pl.ds(x + 1, PX, stride=24), :] = jnp.where(keep, turn(real), imag)

        @pl.loop(1, PX)
        def _(j):
            to = (p + j) % PX
            rows = pl.ds(pl.multiple_of(24 * to, 8), 24)
            here = pl.ds(pl.multiple_of(24 * p, 8), 24)
            push(s1.at[h, rows], r1.at[h, here], px_send.at[0, h], px_recv.at[0, h], to, q).start()

        here = pl.ds(pl.multiple_of(24 * p, 8), 24)
        r1[h, here, :] = s1[h, here, :]

    for copy in far_copies:
        copy.start()

    @pl.when(sends_extra)
    def _():
        extra_copy(SPECIAL, extra_to).start()

    @pl.when(sends_row)
    def _():
        extra_row_copy().start()

    side_copy.wait_recv()
    summed[...] = cover[:, 0:CY]
    summed[:, 0:OV] = summed[:, 0:OV] + side_o[...]
    cover_x = [
        halo(summed.at[pl.ds(0, 24)], low_o, 5, last_p, q),
        halo(summed.at[pl.ds(24, 24)], high_o, 6, next_p, q),
    ]
    for copy in cover_x:
        copy.start()

    def opposite(count):
        places = lax.broadcasted_iota(jnp.int32, (count, count), 0) + lax.broadcasted_iota(jnp.int32, (count, count), 1)
        return places, jnp.where(places == count, 1.0, 0.0)

    flips = opposite(KX)[1].astype(BF16)
    places, lanes_flip = opposite(NY)
    lanes_flip = jnp.where(places == 0, 1.0, lanes_flip).astype(BF16)

    def permute(value):
        high, low = split(value)
        return dot(high, lanes_flip) + dot(low, lanes_flip)

    def mirror(plane, row):
        high, low = split(plane)
        turned = dot(flips, high) + dot(flips, low)
        first_row = lax.broadcasted_iota(jnp.int32, turned.shape, 0) == 0
        return permute(jnp.where(first_row, jnp.broadcast_to(row, turned.shape), turned))

    for copy in near_copies:
        copy.wait_recv()
    gs[0] = 0.5 * (green[1] + mirror(near[...], near_row[0:1]))

    keep = low_lanes((KX, 128))
    special = p == SPECIAL
    most = 31 * 24
    for h in range(2):
        drain(r1.at[h, pl.ds(0, most)], px_recv.at[0, h])
        high, low = split(r1[h])
        both_parts = jnp.concatenate([high, low], axis=1)
        one_h[...] = both_parts

        def rows_body(k, unused):
            rows = pl.ds(pl.multiple_of(KX * k, KX), KX)
            data = one_h[...]
            cosine = dot(cos_h[rows, :], data)
            cosine = cosine[:, :128] + cosine[:, 128:] + dot(cos_l[rows, :], data[:, :128])
            sine = dot(sin_h[rows, :], data)
            sine = sine[:, :128] + sine[:, 128:] + dot(sin_l[rows, :], data[:, :128])
            turned = turn(sine)
            value = jnp.where(keep, cosine + turned, cosine - turned)
            if h == 1:
                below = jnp.where(keep, cosine, -turned)
                above = jnp.where(keep, turn(cosine), -sine)
                parted = jnp.where(k < 4, below, above)
                top = (lax.broadcasted_iota(jnp.int32, (KX, 128), 0) == 0) & (k % 4 == 0)
                value = jnp.where(special & jnp.logical_not(top), parted, jnp.where(special, cosine, value))
            y1[h, k] = value

            @pl.when(k != q)
            def _():
                push(y1.at[h, k], t1.at[h, q], py_send.at[0, h], py_recv.at[0, h], p, k).start()

            return unused

        lax.fori_loop(0, PY, rows_body, 0)
        t1[h, q] = y1[h, q]

    packed = special & (q % 4 == 0)
    top = (lax.broadcasted_iota(jnp.int32, (KX, NY), 0) == 0) & packed

    def second_green():
        for copy in far_copies:
            copy.wait_recv()

        @pl.when(p == SPECIAL)
        def _():
            extra_copy(SPECIAL, extra_to).wait_recv()

        @pl.when((p == SPECIAL) & (q > 4))
        def _():
            extra_row_copy().wait_recv()

        upper = special & (q >= 4)
        lower = special & (q < 4)
        base = jnp.where(p < 16, green[2], jnp.where(lower, extra[...], green[0]))
        plane = jnp.where(upper, extra[...], far[...])
        row = jnp.where(upper, extra_row[0:1], far_row[0:1])
        half = 0.5 * (base + mirror(plane, row))
        packed_rows = jnp.concatenate(
            [jnp.broadcast_to(far_row[0:1], (8, NY)), jnp.broadcast_to(green[0, 0:1], (8, NY))], axis=0
        )
        packed_rows = 0.5 * (packed_rows + permute(packed_rows))
        gs[1] = jnp.where(top, jnp.broadcast_to(packed_rows[0:1], (KX, NY)), half)
        gx[...] = packed_rows[8:16]

    def base_update():
        sublane = lax.broadcasted_iota(jnp.int32, (32, NZ), 0)
        for b in range(boxes):

            def base_body(i, unused):
                value = eta[b, i]
                before = jnp.where(i > 0, eta[b, jnp.maximum(i - 1, 0)], 0.0)
                after = jnp.where(i < 31, eta[b, jnp.minimum(i + 1, 31)], 0.0)
                above = jnp.where(sublane == 0, 0.0, pltpu.roll(value, 1, axis=0))
                below = jnp.where(sublane == 31, 0.0, pltpu.roll(value, 31, axis=0))
                lap = before + after + above + below + pltpu.roll(value, 1, axis=1) + pltpu.roll(value, 127, axis=1)
                lap = lap - 6.0 * value
                square = value * value
                force = value * square - value - 2.0 * COUPLING * value * square - GRADIENT * lap
                result[b, i] = value - RATE * force
                return unused

            lax.fori_loop(0, 32, base_body, 0, unroll=2)

    tables = (table_h[...], table_l[...])
    for h in range(2):
        if h == 1:
            base_update()
            second_green()
        drain(t1.at[h, pl.ds(0, PY - 1)], py_recv.at[0, h])
        for tile in range(4):
            even, odd = t1[h, 2 * tile], t1[h, 2 * tile + 1]
            lanes = slice(128 * tile, 128 * tile + 128)
            work_h[0:96, lanes], work_l[0:96, lanes] = split(jnp.where(keep, even, turn(odd)))
            work_h[96:192, lanes], work_l[96:192, lanes] = split(jnp.where(keep, turn(even), odd))
        wave = dot3((work_h[0:192], work_l[0:192]), tables)
        re_c, re_s = wave[0:96, :NY], wave[0:96, NY:]
        im_c, im_s = wave[96:192, :NY], wave[96:192, NY:]
        real, imag = re_c + im_s, im_c - re_s
        if h == 1:
            real, imag = jnp.where(top, re_c, real), jnp.where(top, -re_s, imag)
            fix = gx[...]
            work_h[192:200], work_l[192:200] = split(fix * im_c[0:8])
            work_h[200:208], work_l[200:208] = split(fix * -im_s[0:8])
        work_h[0:96], work_l[0:96] = split(gs[h] * real)
        work_h[96:192], work_l[96:192] = split(gs[h] * imag)
        used = slice(0, 208 if h == 1 else 192)
        wave = dot3((work_h[used], work_l[used]), tables)
        real = wave[0:96, :NY] - wave[96:192, NY:]
        imag = wave[96:192, :NY] + wave[0:96, NY:]
        if h == 1:
            fix = wave[192:200, :NY] - wave[200:208, NY:]
            imag = jnp.where(top, jnp.broadcast_to(fix[0:1], (KX, NY)), imag)
        for tile in range(4):
            lanes = slice(128 * tile, 128 * tile + 128)
            re, im = real[:, lanes], imag[:, lanes]
            y2[h, 2 * tile] = jnp.where(keep, re, turn(im))
            y2[h, 2 * tile + 1] = jnp.where(keep, turn(re), im)

        @pl.loop(1, PY)
        def _(j):
            to = (q + j) % PY
            push(y2.at[h, to], t2.at[h, q], py_send.at[1, h], py_recv.at[1, h], p, to).start()

        t2[h, q] = y2[h, q]

    for copy in cover_x:
        copy.wait_recv()
    oc_window[0:24, 0:CY] = summed[0:24] + high_o[...]
    oc_window[24:48, 0:CY] = summed[24:48] + low_o[...]
    cover_y = halo(oc_window.at[:, pl.ds(0, OV)], oc_window.at[:, pl.ds(CY, OV)], 7, p, last_q)
    cover_y.start()

    for h in range(2):
        drain(t2.at[h, pl.ds(0, PY - 1)], py_recv.at[1, h])
        for k in range(PY):
            value = t2[h, k]
            turned = turn(value)
            one = value
            two = jnp.where(keep, -turned, turned)
            if h == 1:
                if k < 4:
                    one_s, two_s = jnp.where(keep, 2.0 * value, 0.0), jnp.where(keep, -2.0 * turned, 0.0)
                else:
                    one_s, two_s = jnp.where(keep, 0.0, 2.0 * turned), jnp.where(keep, 0.0, -2.0 * value)
                if k % 4 == 0:
                    row_zero = lax.broadcasted_iota(jnp.int32, (KX, 128), 0) == 0
                    one_s, two_s = jnp.where(row_zero, value, one_s), jnp.where(row_zero, 0.0, two_s)
                one, two = jnp.where(special, one_s, one), jnp.where(special, two_s, two)
            rows = slice(KX * k, KX * k + KX)
            one_h[rows, 0:128], one_h[rows, 128:256] = split(one)
            two_h[rows, 0:128], two_h[rows, 128:256] = split(two)

        def unrows_body(k, unused):
            rows = pl.ds(pl.multiple_of(KX * k, KX), KX)
            one, two = one_h[...], two_h[...]
            result = dot(cos_h[rows, :], one) + dot(sin_h[rows, :], two)
            result = result[:, :128] + result[:, 128:] + dot(cos_l[rows, :], one[:, :128]) + dot(sin_l[rows, :], two[:, :128])
            s2[h, rows, :] = result
            for i in range(4):
                to = 4 * k + i

                @pl.when(to != p)
                def _():
                    part = pl.ds(pl.multiple_of(24 * to, 8), 24)
                    here = pl.ds(pl.multiple_of(24 * p, 8), 24)
                    push(s2.at[h, part], r2.at[h, here], px_send.at[1, h], px_recv.at[1, h], to, q).start()

            return unused

        lax.fori_loop(0, 8, unrows_body, 0)
        here = pl.ds(pl.multiple_of(24 * p, 8), 24)
        r2[h, here, :] = s2[h, here, :]

    keep = low_lanes((PX, 128))
    for h in range(2):
        drain(r2.at[h, pl.ds(0, most)], px_recv.at[1, h])
        waves = (waves_in[256 + 64 * h : 320 + 64 * h], waves_in[384 + 64 * h : 448 + 64 * h])
        for tile in range(CX // 2):
            x = 2 * tile
            even = r2.at[h][pl.ds(x, PX, stride=24), :]
            odd = r2.at[h][pl.ds(x + 1, PX, stride=24), :]
            parts = [jnp.where(keep, even, turn(odd)), jnp.where(keep, turn(even), odd)]
            block = split(jnp.concatenate(parts, axis=0).T)
            value = dot3(block, waves).reshape(2, CY, NZ)
            if h == 0:
                potential[x : x + 2] = value
            else:
                potential[x : x + 2] = potential[x : x + 2] + value

    around = spread(potential, mu_window, 1)
    pending += around
    for copy in around + [cover_y]:
        copy.wait_recv()
    for copy in pending:
        copy.wait_send()

    @pl.when(sends_extra)
    def _():
        extra_copy(SPECIAL, extra_to).wait_send()

    @pl.when(sends_row)
    def _():
        extra_row_copy().wait_send()

    for h in range(2):
        drain(s1.at[h, pl.ds(0, most)], px_send.at[0, h])
        drain(s2.at[h, pl.ds(0, most)], px_send.at[1, h])
        drain(y1.at[h, pl.ds(0, PY - 1)], py_send.at[0, h])
        drain(y2.at[h, pl.ds(0, PY - 1)], py_send.at[1, h])


def place_kernel(corners, ids, misfit, eta, field, cover):
    shift_x, shift_y = lax.axis_index("px") * CX, lax.axis_index("py") * CY
    field[...] = jnp.zeros_like(field)
    cover[...] = jnp.zeros_like(cover)
    for b in range(eta.shape[0]):
        weight = misfit[ids[b]]
        sx = corners[b, 0] * STEP - shift_x
        sy = pl.multiple_of(corners[b, 1] * STEP - shift_y, 8)

        def body(i, unused):
            value = eta[b, i]
            square = value * value
            rows = pl.ds(sy, 32)
            field[sx + i, rows, :] = field[sx + i, rows, :] + weight * square
            cover[sx + i, rows, :] = cover[sx + i, rows, :] + square
            return unused

        lax.fori_loop(0, 32, body, 0, unroll=4)


def final_kernel(corners, ids, misfit, eta, base, mu_window, oc_window, out, potential):
    b = pl.program_id(0)
    shift_x, shift_y = lax.axis_index("px") * CX, lax.axis_index("py") * CY

    @pl.when(b == 0)
    def _():
        potential[...] = mu_window[:CX, :CY]

    factor = 2.0 * RATE * misfit[ids[b]]
    sx = corners[b, 0] * STEP - shift_x
    sy = pl.multiple_of(corners[b, 1] * STEP - shift_y, 8)

    def body(i, unused):
        rows = pl.ds(sy, 32)
        mu = mu_window[sx + i, rows, :]
        total = oc_window[sx + i, rows, :]
        out[0, i] = base[0, i] - eta[0, i] * (2.0 * RATE * COUPLING * total + factor * mu)
        return unused

    lax.fori_loop(0, 32, body, 0, unroll=4)


def on_device(eta, corners, grain_ids, misfit, green):
    forward, inverse = depth_tables()
    dma = pltpu.SemaphoreType.DMA
    arrays = [green, seed_tables(), np.concatenate([*halves(forward), *halves(inverse)])]
    boxes = eta.shape[0]
    vmem = pl.BlockSpec(memory_space=pltpu.VMEM)
    cells = shaped(CX + OV, CY + OV, NZ)
    local = pltpu.CompilerParams(vmem_limit_bytes=24 * 1024 * 1024)
    field, cover = pl.pallas_call(
        place_kernel,
        out_shape=[cells, cells],
        in_specs=[SM] * 3 + [pl.BlockSpec(memory_space=pltpu.VMEM)],
        out_specs=[pl.BlockSpec(memory_space=pltpu.VMEM)] * 2,
        compiler_params=local,
    )(corners, grain_ids, misfit, eta)
    scratch = [
        pltpu.VMEM((NY, 2 * NY), BF16),
        pltpu.VMEM((NY, 2 * NY), BF16),
        pltpu.VMEM((12, CY, NZ), F32),
        pltpu.VMEM((12, CY, NZ), F32),
        pltpu.VMEM((CX + OV, CY, NZ), F32),
        pltpu.VMEM((CX, CY, NZ), F32),
        pltpu.VMEM((2, NX, 128), F32),
        pltpu.VMEM((2, NX, 128), F32),
        *[pltpu.VMEM((2, PY, KX, 128), F32)] * 4,
        pltpu.VMEM((2, NX, 128), F32),
        pltpu.VMEM((2, NX, 128), F32),
        *[pltpu.VMEM((NX, NX), BF16)] * 4,
        *[pltpu.VMEM((KX, NY), F32)] * 3,
        *[pltpu.VMEM((8, NY), F32)] * 3,
        pltpu.VMEM((2, KX, NY), F32),
        pltpu.VMEM((8, NY), F32),
        *[pltpu.VMEM((208, NY), BF16)] * 2,
        *[pltpu.VMEM((NX, 256), BF16)] * 2,
        pltpu.VMEM((CX, CY, NZ), F32),
        pltpu.VMEM((CX + OV, 8, NZ), F32),
        pltpu.VMEM((CX + OV, 16, NZ), F32),
        pltpu.VMEM((12, CY, NZ), F32),
        pltpu.VMEM((12, CY, NZ), F32),
        pltpu.VMEM((CX + OV, OV, NZ), F32),
        pltpu.VMEM((24, CY, NZ), F32),
        pltpu.VMEM((24, CY, NZ), F32),
        dma((2, 8)),
        dma((2, 8)),
        dma((6,)),
        dma((6,)),
        *[dma((2, 2))] * 4,
    ]
    base, mu, total = pl.pallas_call(
        mega_kernel,
        out_shape=[shaped(*eta.shape), cells, cells],
        in_specs=[vmem] * (3 + len(arrays)),
        out_specs=[vmem] * 3,
        scratch_shapes=scratch,
        compiler_params=pltpu.CompilerParams(
            vmem_limit_bytes=36 * 1024 * 1024, collective_id=0, has_side_effects=True
        ),
    )(eta, field, cover, *arrays)
    block = pl.BlockSpec((1, 32, 32, NZ), lambda b: (b, 0, 0, 0))
    window = pl.BlockSpec((CX + OV, CY + OV, NZ), lambda b: (0, 0, 0))
    return pl.pallas_call(
        final_kernel,
        grid=(boxes,),
        out_shape=[shaped(*eta.shape), shaped(CX, CY, NZ)],
        in_specs=[SM] * 3 + [block, block, window, window],
        out_specs=[block, pl.BlockSpec((CX, CY, NZ), lambda b: (0, 0, 0))],
        compiler_params=local,
    )(corners, grain_ids, misfit, eta, base, mu, total)


def solution(mesh):
    in_specs = (P(("px", "py"), None, None, None), P(("px", "py"), None), P(("px", "py")), P(), P("px", "py", None))
    out_specs = (P(("px", "py"), None, None, None), P("px", "py", None))
    return jax.shard_map(on_device, mesh=mesh, in_specs=in_specs, out_specs=out_specs, check_vma=False)
```

```python
import functools

import jax
import jax.numpy as jnp
import numpy as np
from jax import lax
from jax.experimental import pallas as pl
from jax.experimental.pallas import tpu as pltpu
from jax.sharding import PartitionSpec as P

NX, NY, NZ = 768, 512, 128
STEP = 8
PX, PY = 32, 8
CX, CY = NX // PX, NY // PY
OV = 24
KX = NX // PY
F32 = jnp.float32
BF16 = jnp.bfloat16
SPECIAL = 16
RATE = 0.2
GRADIENT = 0.1
COUPLING = 1.5

SM = pl.BlockSpec(memory_space=pltpu.SMEM)


def halves(array):
    high = np.asarray(array, np.float32).astype(jnp.bfloat16)
    low = (np.asarray(array, np.float64) - high.astype(np.float64)).astype(jnp.bfloat16)
    return high, low


def slot_wave(p, h):
    if h == 0:
        return 4 * p + 1
    return 4 * p + 2 if p < 16 else 4 * p


def depth_tables():
    z = np.arange(NZ)
    forward = np.zeros((NZ, NZ))
    inverse = np.zeros((NZ, NZ))
    total = NX * NY * NZ
    for h in range(2):
        for p in range(PX):
            row_re, row_im = h * 64 + p, h * 64 + 32 + p
            wave = slot_wave(p, h)
            cosine = np.cos(2 * np.pi * ((wave * z) % NZ) / NZ)
            sine = np.sin(2 * np.pi * ((wave * z) % NZ) / NZ)
            if p == SPECIAL and h == 1:
                forward[row_re], forward[row_im] = 1.0, (-1.0) ** z
                inverse[row_re], inverse[row_im] = 1.0 / total, (-1.0) ** z / total
            else:
                forward[row_re], forward[row_im] = cosine, -sine
                inverse[row_re], inverse[row_im] = 2 * cosine / total, -2 * sine / total
    return forward, inverse


def wave_rows(count, step, length):
    angle = 2 * np.pi * ((step * np.arange(count)[:, None] * np.arange(length)[None]) % length) / length
    return np.stack([np.cos(angle), np.sin(angle)]).astype(np.float32)


def seed_tables():
    seeds = np.zeros((2, 104, NX), np.float32)
    seeds[:, 0:24] = wave_rows(24, 32, NX)
    seeds[:, 24:56] = wave_rows(32, 1, NX)
    seeds[:, 56:72, :NY] = wave_rows(16, 32, NY)
    seeds[:, 72:104, :NY] = wave_rows(32, 1, NY)
    return seeds


def split(value):
    high = value.astype(BF16)
    return high, (value - high.astype(F32)).astype(BF16)


def dot(a, b):
    return jnp.dot(a, b, preferred_element_type=F32)


def dot3(a, b):
    return dot(a[0], b[0]) + dot(a[0], b[1]) + dot(a[1], b[0])


def turn(value):
    return pltpu.roll(value, 64, axis=value.ndim - 1)


def low_lanes(shape):
    return lax.broadcasted_iota(jnp.int32, shape, len(shape) - 1) < 64


def shaped(*shape, dtype=F32):
    return jax.ShapeDtypeStruct(shape, dtype)


MESH = pl.DeviceIdType.MESH
CUT_X = ((0, 12), (12, 36), (36, 48))
CUT_Y = ((0, 8), (8, 72), (72, 88))
TAKE_X = ((0, 12), (0, 24), (12, 24))
TAKE_Y = ((0, 16), (0, 64), (56, 64))
GIVE_X = ((36, 48), (12, 36), (0, 12))
GIVE_Y = ((72, 88), (8, 72), (0, 8))
AROUND = [(a, b) for a, b in ((0, 1), (2, 1), (1, 0), (1, 2), (0, 0), (0, 2), (2, 0), (2, 2))]


def box(ref, x, y):
    return ref.at[pl.ds(x[0], x[1] - x[0]), pl.ds(y[0], y[1] - y[0])]


def wrap(value, count):
    return (value + count) % count


def push(source, target, send, receive, p, q):
    return pltpu.make_async_remote_copy(
        src_ref=source, dst_ref=target, send_sem=send, recv_sem=receive, device_id=(p, q), device_id_type=MESH
    )


def drain(ref, semaphore):
    pltpu.make_async_copy(ref, ref, semaphore).wait()


def mega_kernel(
    eta, field, cover, green, seeds, waves_in,
    result, mu_window, oc_window,
    table_h, table_l, cut_low, cut_high, summed,
    grid, s1, r1, y1, t1, y2, t2, s2, r2, cos_h, cos_l, sin_h, sin_l,
    near, far, extra, near_row, far_row, extra_row, gs, gx, work_h, work_l, one_h, two_h, potential,
    low_y, high_y, low_x, high_x, side_o, low_o, high_o, halo_send, halo_recv, green_send, green_recv, px_send, px_recv, py_send, py_recv,
):
    p, q = lax.axis_index("px"), lax.axis_index("py")
    upper_half = p // 16
    far_to = 31 - p + (1 - upper_half) - 16 * (1 - (p + 31) // 32)
    far_from = 31 - p + upper_half - 16 * upper_half * (1 - (p + 15) // 32)
    flip, flip_row = 7 - q, (8 - q) % 8

    boxes = eta.shape[0]
    barrier = pltpu.get_barrier_semaphore()

    def greet(a, b):
        pl.semaphore_signal(barrier, inc=1, device_id=(a, b), device_id_type=MESH)

    @pl.loop(1, PX)
    def _(j):
        greet((p + j) % PX, q)

    @pl.loop(1, PY)
    def _(j):
        greet(p, (q + j) % PY)

    for a in (-1, 1):
        for b in (-1, 1):
            greet(wrap(p + a, PX), wrap(q + b, PY))
    greet(31 - p, flip)
    greet(31 - p, flip_row)
    greet(far_from, flip)
    greet(far_from, flip_row)
    pl.semaphore_wait(barrier, (PX - 1) + (PY - 1) + 8)

    def spread(source, window, group):
        copies = []
        for n, (a, b) in enumerate(AROUND):
            copy = push(
                box(source, TAKE_X[a], TAKE_Y[b]), box(window, GIVE_X[a], GIVE_Y[b]),
                halo_send.at[group, n], halo_recv.at[group, n], wrap(p + a - 1, PX), wrap(q + b - 1, PY),
            )
            copy.start()
            copies.append(copy)
        box(window, CUT_X[1], CUT_Y[1])[...] = source[...]
        return copies

    near_copies = [
        push(green.at[3], near, green_send.at[0], green_recv.at[0], 31 - p, flip),
        push(green.at[3, pl.ds(0, 8)], near_row, green_send.at[2], green_recv.at[2], 31 - p, flip_row),
    ]
    far_copies = [
        push(green.at[2 * upper_half], far, green_send.at[1], green_recv.at[1], far_to, flip),
        push(green.at[2 * upper_half, pl.ds(0, 8)], far_row, green_send.at[3], green_recv.at[3], far_to, flip_row),
    ]
    for copy in near_copies:
        copy.start()
    pending = near_copies + far_copies
    next_p, last_p, next_q, last_q = wrap(p + 1, PX), wrap(p - 1, PX), wrap(q + 1, PY), wrap(q - 1, PY)

    def halo(source, target, slot, a, b):
        copy = push(source, target, halo_send.at[0, slot], halo_recv.at[0, slot], a, b)
        pending.append(copy)
        return copy

    along_y = [
        halo(field.at[:, pl.ds(0, 8)], low_y, 0, p, last_q),
        halo(field.at[:, pl.ds(72, 16)], high_y, 1, p, next_q),
    ]
    for copy in along_y:
        copy.start()
    side_copy = halo(cover.at[:, pl.ds(CY, OV)], side_o, 2, p, next_q)
    side_copy.start()
    for copy in along_y:
        copy.wait_recv()

    def joined(target, rows):
        target[...] = field[rows, 8 : 8 + CY]
        target[:, 0:16] = target[:, 0:16] + high_y[rows]
        target[:, 56:64] = target[:, 56:64] + low_y[rows]

    joined(cut_low, slice(0, 12))
    joined(cut_high, slice(36, 48))
    along_x = [halo(cut_low, low_x, 3, last_p, q), halo(cut_high, high_x, 4, next_p, q)]
    for copy in along_x:
        copy.start()
    joined(grid, slice(12, 36))

    def extra_copy(a, b):
        return push(green.at[0], extra, green_send.at[4], green_recv.at[4], a, b)

    def extra_row_copy():
        return push(green.at[0, pl.ds(0, 8)], extra_row, green_send.at[5], green_recv.at[5], SPECIAL, flip_row)

    sends_extra = ((p == 0) | (p == SPECIAL)) & (q < 4)
    sends_row = (p == SPECIAL) & (q > 0) & (q < 4)
    extra_to = q + (p // SPECIAL) * (flip - q)

    fine_c, fine_s = seeds[0, 24:56], seeds[1, 24:56]

    def table_body(k, unused):
        coarse_c, coarse_s = seeds[0, pl.ds(k, 1), :], seeds[1, pl.ds(k, 1), :]
        rows = pl.ds(pl.multiple_of(32 * k, 32), 32)
        cos_h[rows, :], cos_l[rows, :] = split(coarse_c * fine_c - coarse_s * fine_s)
        sin_h[rows, :], sin_l[rows, :] = split(coarse_s * fine_c + coarse_c * fine_s)
        return unused

    lax.fori_loop(0, NX // 32, table_body, 0)
    short_c, short_s = seeds[0, 72:104, :NY], seeds[1, 72:104, :NY]

    def column_body(k, unused):
        coarse_c, coarse_s = seeds[0, pl.ds(56 + k, 1), :NY], seeds[1, pl.ds(56 + k, 1), :NY]
        rows = pl.ds(pl.multiple_of(32 * k, 32), 32)
        table_h[rows, 0:NY], table_l[rows, 0:NY] = split(coarse_c * short_c - coarse_s * short_s)
        table_h[rows, NY:], table_l[rows, NY:] = split(coarse_s * short_c + coarse_c * short_s)
        return unused

    lax.fori_loop(0, NY // 32, column_body, 0)

    for copy in along_x:
        copy.wait_recv()
    grid[0:12] = grid[0:12] + high_x[...]
    grid[12:24] = grid[12:24] + low_x[...]

    side_copy.wait_recv()
    summed[...] = cover[:, 0:CY]
    summed[:, 0:OV] = summed[:, 0:OV] + side_o[...]
    cover_x = [
        halo(summed.at[pl.ds(0, 24)], low_o, 5, last_p, q),
        halo(summed.at[pl.ds(24, 24)], high_o, 6, next_p, q),
    ]
    for copy in cover_x:
        copy.start()

    keep = low_lanes((PX, 128))
    nt = (((1,), (1,)), ((), ()))
    for h in range(2):
        waves = (waves_in[64 * h : 64 * h + 64], waves_in[128 + 64 * h : 192 + 64 * h])
        for group in range(CX // 4):
            rows = split(grid[4 * group : 4 * group + 4].reshape(256, NZ))
            spectrum = (
                lax.dot_general(waves[0], rows[0], nt, preferred_element_type=F32)
                + lax.dot_general(waves[0], rows[1], nt, preferred_element_type=F32)
                + lax.dot_general(waves[1], rows[0], nt, preferred_element_type=F32)
            )
            for tile in range(2):
                real = spectrum[0:32, 128 * tile : 128 * tile + 128]
                imag = spectrum[32:64, 128 * tile : 128 * tile + 128]
                x = 4 * group + 2 * tile
                s1.at[h][pl.ds(x, PX, stride=24), :] = jnp.where(keep, real, turn(imag))
                s1.at[h][pl.ds(x + 1, PX, stride=24), :] = jnp.where(keep, turn(real), imag)

        @pl.loop(1, PX)
        def _(j):
            to = (p + j) % PX
            rows = pl.ds(pl.multiple_of(24 * to, 8), 24)
            here = pl.ds(pl.multiple_of(24 * p, 8), 24)
            push(s1.at[h, rows], r1.at[h, here], px_send.at[0, h], px_recv.at[0, h], to, q).start()

        here = pl.ds(pl.multiple_of(24 * p, 8), 24)
        r1[h, here, :] = s1[h, here, :]

    for copy in far_copies:
        copy.start()

    @pl.when(sends_extra)
    def _():
        extra_copy(SPECIAL, extra_to).start()

    @pl.when(sends_row)
    def _():
        extra_row_copy().start()

    def opposite(count):
        places = lax.broadcasted_iota(jnp.int32, (count, count), 0) + lax.broadcasted_iota(jnp.int32, (count, count), 1)
        return places, jnp.where(places == count, 1.0, 0.0)

    flips = opposite(KX)[1].astype(BF16)
    places, lanes_flip = opposite(NY)
    lanes_flip = jnp.where(places == 0, 1.0, lanes_flip).astype(BF16)

    def permute(value):
        high, low = split(value)
        return dot(high, lanes_flip) + dot(low, lanes_flip)

    def mirror(plane, row):
        high, low = split(plane)
        turned = dot(flips, high) + dot(flips, low)
        first_row = lax.broadcasted_iota(jnp.int32, turned.shape, 0) == 0
        return permute(jnp.where(first_row, jnp.broadcast_to(row, turned.shape), turned))

    for copy in near_copies:
        copy.wait_recv()
    gs[0] = 0.5 * (green[1] + mirror(near[...], near_row[0:1]))

    keep = low_lanes((KX, 128))
    special = p == SPECIAL
    most = 31 * 24
    for h in range(2):
        drain(r1.at[h, pl.ds(0, most)], px_recv.at[0, h])
        high, low = split(r1[h])
        both_parts = jnp.concatenate([high, low], axis=1)
        one_h[...] = both_parts

        def rows_body(k, unused):
            rows = pl.ds(pl.multiple_of(KX * k, KX), KX)
            data = one_h[...]
            cosine = dot(cos_h[rows, :], data)
            cosine = cosine[:, :128] + cosine[:, 128:] + dot(cos_l[rows, :], data[:, :128])
            sine = dot(sin_h[rows, :], data)
            sine = sine[:, :128] + sine[:, 128:] + dot(sin_l[rows, :], data[:, :128])
            turned = turn(sine)
            value = jnp.where(keep, cosine + turned, cosine - turned)
            if h == 1:
                below = jnp.where(keep, cosine, -turned)
                above = jnp.where(keep, turn(cosine), -sine)
                parted = jnp.where(k < 4, below, above)
                top = (lax.broadcasted_iota(jnp.int32, (KX, 128), 0) == 0) & (k % 4 == 0)
                value = jnp.where(special & jnp.logical_not(top), parted, jnp.where(special, cosine, value))
            y1[h, k] = value

            @pl.when(k != q)
            def _():
                push(y1.at[h, k], t1.at[h, q], py_send.at[0, h], py_recv.at[0, h], p, k).start()

            return unused

        lax.fori_loop(0, PY, rows_body, 0)
        t1[h, q] = y1[h, q]

    packed = special & (q % 4 == 0)
    top = (lax.broadcasted_iota(jnp.int32, (KX, NY), 0) == 0) & packed

    def second_green():
        for copy in far_copies:
            copy.wait_recv()

        @pl.when(p == SPECIAL)
        def _():
            extra_copy(SPECIAL, extra_to).wait_recv()

        @pl.when((p == SPECIAL) & (q > 4))
        def _():
            extra_row_copy().wait_recv()

        upper = special & (q >= 4)
        lower = special & (q < 4)
        base = jnp.where(p < 16, green[2], jnp.where(lower, extra[...], green[0]))
        plane = jnp.where(upper, extra[...], far[...])
        row = jnp.where(upper, extra_row[0:1], far_row[0:1])
        half = 0.5 * (base + mirror(plane, row))
        packed_rows = jnp.concatenate(
            [jnp.broadcast_to(far_row[0:1], (8, NY)), jnp.broadcast_to(green[0, 0:1], (8, NY))], axis=0
        )
        packed_rows = 0.5 * (packed_rows + permute(packed_rows))
        gs[1] = jnp.where(top, jnp.broadcast_to(packed_rows[0:1], (KX, NY)), half)
        gx[...] = packed_rows[8:16]

    tables = (table_h[...], table_l[...])
    for h in range(2):
        if h == 1:
            second_green()
        drain(t1.at[h, pl.ds(0, PY - 1)], py_recv.at[0, h])
        for tile in range(4):
            even, odd = t1[h, 2 * tile], t1[h, 2 * tile + 1]
            lanes = slice(128 * tile, 128 * tile + 128)
            work_h[0:96, lanes], work_l[0:96, lanes] = split(jnp.where(keep, even, turn(odd)))
            work_h[96:192, lanes], work_l[96:192, lanes] = split(jnp.where(keep, turn(even), odd))
        wave = dot3((work_h[0:192], work_l[0:192]), tables)
        re_c, re_s = wave[0:96, :NY], wave[0:96, NY:]
        im_c, im_s = wave[96:192, :NY], wave[96:192, NY:]
        real, imag = re_c + im_s, im_c - re_s
        if h == 1:
            real, imag = jnp.where(top, re_c, real), jnp.where(top, -re_s, imag)
            fix = gx[...]
            work_h[192:200], work_l[192:200] = split(fix * im_c[0:8])
            work_h[200:208], work_l[200:208] = split(fix * -im_s[0:8])
        work_h[0:96], work_l[0:96] = split(gs[h] * real)
        work_h[96:192], work_l[96:192] = split(gs[h] * imag)
        used = slice(0, 208 if h == 1 else 192)
        wave = dot3((work_h[used], work_l[used]), tables)
        real = wave[0:96, :NY] - wave[96:192, NY:]
        imag = wave[96:192, :NY] + wave[0:96, NY:]
        if h == 1:
            fix = wave[192:200, :NY] - wave[200:208, NY:]
            imag = jnp.where(top, jnp.broadcast_to(fix[0:1], (KX, NY)), imag)
        for tile in range(4):
            lanes = slice(128 * tile, 128 * tile + 128)
            re, im = real[:, lanes], imag[:, lanes]
            y2[h, 2 * tile] = jnp.where(keep, re, turn(im))
            y2[h, 2 * tile + 1] = jnp.where(keep, turn(re), im)

        @pl.loop(1, PY)
        def _(j):
            to = (q + j) % PY
            push(y2.at[h, to], t2.at[h, q], py_send.at[1, h], py_recv.at[1, h], p, to).start()

        t2[h, q] = y2[h, q]

    for copy in cover_x:
        copy.wait_recv()
    oc_window[0:24, 0:CY] = summed[0:24] + high_o[...]
    oc_window[24:48, 0:CY] = summed[24:48] + low_o[...]
    cover_y = halo(oc_window.at[:, pl.ds(0, OV)], oc_window.at[:, pl.ds(CY, OV)], 7, p, last_q)
    cover_y.start()

    for h in range(2):
        drain(t2.at[h, pl.ds(0, PY - 1)], py_recv.at[1, h])
        for k in range(PY):
            value = t2[h, k]
            turned = turn(value)
            one = value
            two = jnp.where(keep, -turned, turned)
            if h == 1:
                if k < 4:
                    one_s, two_s = jnp.where(keep, 2.0 * value, 0.0), jnp.where(keep, -2.0 * turned, 0.0)
                else:
                    one_s, two_s = jnp.where(keep, 0.0, 2.0 * turned), jnp.where(keep, 0.0, -2.0 * value)
                if k % 4 == 0:
                    row_zero = lax.broadcasted_iota(jnp.int32, (KX, 128), 0) == 0
                    one_s, two_s = jnp.where(row_zero, value, one_s), jnp.where(row_zero, 0.0, two_s)
                one, two = jnp.where(special, one_s, one), jnp.where(special, two_s, two)
            rows = slice(KX * k, KX * k + KX)
            one_h[rows, 0:128], one_h[rows, 128:256] = split(one)
            two_h[rows, 0:128], two_h[rows, 128:256] = split(two)

        def unrows_body(k, unused):
            rows = pl.ds(pl.multiple_of(KX * k, KX), KX)
            one, two = one_h[...], two_h[...]
            result = dot(cos_h[rows, :], one) + dot(sin_h[rows, :], two)
            result = result[:, :128] + result[:, 128:] + dot(cos_l[rows, :], one[:, :128]) + dot(sin_l[rows, :], two[:, :128])
            s2[h, rows, :] = result
            for i in range(4):
                to = 4 * k + i

                @pl.when(to != p)
                def _():
                    part = pl.ds(pl.multiple_of(24 * to, 8), 24)
                    here = pl.ds(pl.multiple_of(24 * p, 8), 24)
                    push(s2.at[h, part], r2.at[h, here], px_send.at[1, h], px_recv.at[1, h], to, q).start()

            return unused

        lax.fori_loop(0, 8, unrows_body, 0)
        here = pl.ds(pl.multiple_of(24 * p, 8), 24)
        r2[h, here, :] = s2[h, here, :]

    cover_y.wait_recv()
    sublane = lax.broadcasted_iota(jnp.int32, (32, NZ), 0)
    for b in range(boxes):

        def base_body(i, unused):
            value = eta[b, i]
            before = jnp.where(i > 0, eta[b, jnp.maximum(i - 1, 0)], 0.0)
            after = jnp.where(i < 31, eta[b, jnp.minimum(i + 1, 31)], 0.0)
            above = jnp.where(sublane == 0, 0.0, pltpu.roll(value, 1, axis=0))
            below = jnp.where(sublane == 31, 0.0, pltpu.roll(value, 31, axis=0))
            lap = before + after + above + below + pltpu.roll(value, 1, axis=1) + pltpu.roll(value, 127, axis=1)
            lap = lap - 6.0 * value
            square = value * value
            force = value * square - value - 2.0 * COUPLING * value * square - GRADIENT * lap
            result[b, i] = value - RATE * force
            return unused

        lax.fori_loop(0, 32, base_body, 0, unroll=2)

    keep = low_lanes((PX, 128))
    for h in range(2):
        drain(r2.at[h, pl.ds(0, most)], px_recv.at[1, h])
        waves = (waves_in[256 + 64 * h : 320 + 64 * h], waves_in[384 + 64 * h : 448 + 64 * h])
        for tile in range(CX // 2):
            x = 2 * tile
            even = r2.at[h][pl.ds(x, PX, stride=24), :]
            odd = r2.at[h][pl.ds(x + 1, PX, stride=24), :]
            parts = [jnp.where(keep, even, turn(odd)), jnp.where(keep, turn(even), odd)]
            block = split(jnp.concatenate(parts, axis=0).T)
            value = dot3(block, waves).reshape(2, CY, NZ)
            if h == 0:
                potential[x : x + 2] = value
            else:
                potential[x : x + 2] = potential[x : x + 2] + value

    around = spread(potential, mu_window, 1)
    pending += around
    for copy in around:
        copy.wait_recv()
    for copy in pending:
        copy.wait_send()

    @pl.when(sends_extra)
    def _():
        extra_copy(SPECIAL, extra_to).wait_send()

    @pl.when(sends_row)
    def _():
        extra_row_copy().wait_send()

    for h in range(2):
        drain(s1.at[h, pl.ds(0, most)], px_send.at[0, h])
        drain(s2.at[h, pl.ds(0, most)], px_send.at[1, h])
        drain(y1.at[h, pl.ds(0, PY - 1)], py_send.at[0, h])
        drain(y2.at[h, pl.ds(0, PY - 1)], py_send.at[1, h])


def place_kernel(corners, ids, misfit, eta, field, cover):
    shift_x, shift_y = lax.axis_index("px") * CX, lax.axis_index("py") * CY
    field[...] = jnp.zeros_like(field)
    cover[...] = jnp.zeros_like(cover)
    for b in range(eta.shape[0]):
        weight = misfit[ids[b]]
        sx = corners[b, 0] * STEP - shift_x
        sy = pl.multiple_of(corners[b, 1] * STEP - shift_y, 8)

        def body(i, unused):
            value = eta[b, i]
            square = value * value
            rows = pl.ds(sy, 32)
            field[sx + i, rows, :] = field[sx + i, rows, :] + weight * square
            cover[sx + i, rows, :] = cover[sx + i, rows, :] + square
            return unused

        lax.fori_loop(0, 32, body, 0, unroll=4)


def final_kernel(corners, ids, misfit, eta, base, mu_window, oc_window, out, potential):
    b = pl.program_id(0)
    shift_x, shift_y = lax.axis_index("px") * CX, lax.axis_index("py") * CY

    @pl.when(b == 0)
    def _():
        potential[...] = mu_window[:CX, :CY]

    factor = 2.0 * RATE * misfit[ids[b]]
    sx = corners[b, 0] * STEP - shift_x
    sy = pl.multiple_of(corners[b, 1] * STEP - shift_y, 8)

    def body(i, unused):
        rows = pl.ds(sy, 32)
        mu = mu_window[sx + i, rows, :]
        total = oc_window[sx + i, rows, :]
        out[0, i] = base[0, i] - eta[0, i] * (2.0 * RATE * COUPLING * total + factor * mu)
        return unused

    lax.fori_loop(0, 32, body, 0, unroll=4)


def on_device(eta, corners, grain_ids, misfit, green):
    forward, inverse = depth_tables()
    dma = pltpu.SemaphoreType.DMA
    arrays = [green, seed_tables(), np.concatenate([*halves(forward), *halves(inverse)])]
    boxes = eta.shape[0]
    vmem = pl.BlockSpec(memory_space=pltpu.VMEM)
    cells = shaped(CX + OV, CY + OV, NZ)
    local = pltpu.CompilerParams(vmem_limit_bytes=24 * 1024 * 1024)
    field, cover = pl.pallas_call(
        place_kernel,
        out_shape=[cells, cells],
        in_specs=[SM] * 3 + [pl.BlockSpec(memory_space=pltpu.VMEM)],
        out_specs=[pl.BlockSpec(memory_space=pltpu.VMEM)] * 2,
        compiler_params=local,
    )(corners, grain_ids, misfit, eta)
    scratch = [
        pltpu.VMEM((NY, 2 * NY), BF16),
        pltpu.VMEM((NY, 2 * NY), BF16),
        pltpu.VMEM((12, CY, NZ), F32),
        pltpu.VMEM((12, CY, NZ), F32),
        pltpu.VMEM((CX + OV, CY, NZ), F32),
        pltpu.VMEM((CX, CY, NZ), F32),
        pltpu.VMEM((2, NX, 128), F32),
        pltpu.VMEM((2, NX, 128), F32),
        *[pltpu.VMEM((2, PY, KX, 128), F32)] * 4,
        pltpu.VMEM((2, NX, 128), F32),
        pltpu.VMEM((2, NX, 128), F32),
        *[pltpu.VMEM((NX, NX), BF16)] * 4,
        *[pltpu.VMEM((KX, NY), F32)] * 3,
        *[pltpu.VMEM((8, NY), F32)] * 3,
        pltpu.VMEM((2, KX, NY), F32),
        pltpu.VMEM((8, NY), F32),
        *[pltpu.VMEM((208, NY), BF16)] * 2,
        *[pltpu.VMEM((NX, 256), BF16)] * 2,
        pltpu.VMEM((CX, CY, NZ), F32),
        pltpu.VMEM((CX + OV, 8, NZ), F32),
        pltpu.VMEM((CX + OV, 16, NZ), F32),
        pltpu.VMEM((12, CY, NZ), F32),
        pltpu.VMEM((12, CY, NZ), F32),
        pltpu.VMEM((CX + OV, OV, NZ), F32),
        pltpu.VMEM((24, CY, NZ), F32),
        pltpu.VMEM((24, CY, NZ), F32),
        dma((2, 8)),
        dma((2, 8)),
        dma((6,)),
        dma((6,)),
        *[dma((2, 2))] * 4,
    ]
    base, mu, total = pl.pallas_call(
        mega_kernel,
        out_shape=[shaped(*eta.shape), cells, cells],
        in_specs=[vmem] * (3 + len(arrays)),
        out_specs=[vmem] * 3,
        scratch_shapes=scratch,
        compiler_params=pltpu.CompilerParams(
            vmem_limit_bytes=36 * 1024 * 1024, collective_id=0, has_side_effects=True
        ),
    )(eta, field, cover, *arrays)
    block = pl.BlockSpec((1, 32, 32, NZ), lambda b: (b, 0, 0, 0))
    window = pl.BlockSpec((CX + OV, CY + OV, NZ), lambda b: (0, 0, 0))
    return pl.pallas_call(
        final_kernel,
        grid=(boxes,),
        out_shape=[shaped(*eta.shape), shaped(CX, CY, NZ)],
        in_specs=[SM] * 3 + [block, block, window, window],
        out_specs=[block, pl.BlockSpec((CX, CY, NZ), lambda b: (0, 0, 0))],
        compiler_params=local,
    )(corners, grain_ids, misfit, eta, base, mu, total)


def solution(mesh):
    in_specs = (P(("px", "py"), None, None, None), P(("px", "py"), None), P(("px", "py")), P(), P("px", "py", None))
    out_specs = (P(("px", "py"), None, None, None), P("px", "py", None))
    return jax.shard_map(on_device, mesh=mesh, in_specs=in_specs, out_specs=out_specs, check_vma=False)
```
